32 devices in a mesh: row: 8 (over z, y), col: 4 (over x, core).
Axes of the slice: x: 2, y: 2, z: 4, core: 2. Of those that a mesh axis runs over, the one named last changes fastest.
Arguments:
- obs_panel: bfloat16 [196608, 2048], P('row', 'col'), may hold values from -0.1875 to 0.1875
- skies: bfloat16 [196608, 256], P('row', 'col'), may hold values from -6 to 6
- panel_index: int32 [2048], replicated, may hold values from 0 to 196607
- prior_sum: float32 [196608, 256], P('row', 'col'), may hold values from -6 to 6
- apod: float32 [196608], P('row'), may hold values from 0.05 to 1
- proj_panel: bfloat16 [2048, 196608], P(None, ('row', 'col')), may hold values from -0.02734375 to 0.02734375
Outputs:
- reobserved: float32 [196608, 256], P('row', 'col')
- projection: float32 [2048, 256], P('row', 'col')
The draws below stay inside these ranges and needn't reach their ends.
Inputs may be any that keep to these rules, and one draw needn't show every extreme that they name: `panel_index`: rows of the observed patch; a row may appear more than once.
All inputs are finite; a program needn't handle non-finite values.
Results may differ from the reference program's by a relative error of at most 0.0029.
Values may be sent and summed in bfloat16 or wider, within the bound.
A program may use at most 192 MiB of HBM per device.

```python
import math
import jax
import jax.numpy as jnp

NP = 196608
PANEL = 2048
NSIM = 256
PROWS = 2048


def set_ends(array, own_key, least, top_value):
    spot = [jax.random.randint(jax.random.fold_in(own_key, axis), (), 0, length) for axis, length in enumerate(array.shape)]
    longest = array.shape.index(max(array.shape))
    next_to = spot[:longest] + [(spot[longest] + 1) % array.shape[longest]] + spot[longest + 1:]
    return array.at[tuple(spot)].set(least).at[tuple(next_to)].set(top_value)


def with_spikes(entries, own_key, source, target, parts, factor):
    owner, partner = [(jnp.arange(entries.shape[dim]) // (entries.shape[dim] // parts)).reshape([-1 if axis == dim else 1 for axis in range(entries.ndim)]) for dim in (source, target)]
    chosen = jax.random.permutation(own_key, parts)[partner]
    strong = (owner == chosen) | (owner == (partner + parts // 2) % parts)
    return jnp.where(strong, factor * entries, entries)


def block_scale(key, dims, shards, low, largest):
    loudness, own = 1.0, jax.random.fold_in(key, 6)
    for axis_at, blocks in shards:
        steps = jnp.exp(jax.random.uniform(jax.random.fold_in(own, axis_at), (blocks,), jnp.float32, low / len(shards), largest / len(shards)))
        loudness = loudness * jnp.repeat(steps, dims[axis_at] // blocks).reshape([-1 if axis == axis_at else 1 for axis in range(len(dims))])
    return loudness


def bell_draw(own_key, dims, deviation, bound, split=(), dtype=jnp.bfloat16):
    result = jax.random.normal(own_key, dims, jnp.float32) * deviation
    if len(split) > 0:
        result = block_scale(own_key, dims, split, -0.22, 0.18) * result
    return jnp.clip(result, min=-bound, max=bound).astype(dtype)


def gaussian_with(own_key, extent, width, most, pieces, heavy, held_as=jnp.bfloat16):
    values = width * jax.random.normal(own_key, extent, jnp.float32)
    if pieces:
        values = values * block_scale(own_key, extent, pieces, -0.22, 0.18)
    return jnp.clip(with_spikes(values, jax.random.fold_in(own_key, 3), *heavy), -most, most).astype(held_as)


def setup_inputs(seed: int = 0) -> dict:
    arg_keys = jax.random.split(jax.random.key(seed), 7)
    return {
        "obs_panel": gaussian_with(arg_keys[0], (NP, PANEL), PANEL ** -0.5, 0.1875, ((0, 8), (1, 4)), (1, 0, 8, 2.0)),
        "skies": bell_draw(arg_keys[1], (NP, NSIM), 1.0, 6.0, ((0, 8), (1, 4))),
        "panel_index": set_ends(jax.random.randint(arg_keys[2], (PANEL,), 0, NP), jax.random.fold_in(arg_keys[2], 1), 0, NP - 1).astype(jnp.int32),
        "prior_sum": bell_draw(arg_keys[3], (NP, NSIM), 1.0, 6.0, ((0, 8), (1, 4)), jnp.float32),
        "apod": jnp.clip(jnp.exp(math.log(1.0) - 2.9957323 * jax.random.uniform(arg_keys[4], (NP,), jnp.float32) ** block_scale(arg_keys[4], (NP,), ((0, 8),), -0.2, 0.2)), 0.05, 1.0),
        "proj_panel": gaussian_with(arg_keys[5], (PROWS, NP), NP ** -0.5, 0.02734375, ((1, 32),), (1, 0, 32, 2.75)),
    }


def reference(obs_panel, skies, panel_index, prior_sum, apod, proj_panel):
    picked = jnp.take(skies, panel_index, axis=0)
    reobserved = prior_sum + jnp.dot(obs_panel, picked, preferred_element_type=jnp.float32)
    weighted = (apod[:, None] * reobserved).astype(jnp.bfloat16)
    projection = jnp.dot(proj_panel, weighted, preferred_element_type=jnp.float32)
    return reobserved, projection
```

```python
import functools
import math

import jax
import jax.numpy as jnp
from jax import lax
from jax.experimental import pallas as pl
from jax.experimental.pallas import tpu as pltpu
from jax.sharding import PartitionSpec as P

MESH = pl.DeviceIdType.MESH
NT = (((1,), (1,)), ((), ()))
UNIT = 256
D2, D3 = 1, 4
IN, SENDS = 3, 3
LIMIT = 48 * 1024 * 1024


def remote(src, dst, send, recv, row, col):
    return pltpu.make_async_remote_copy(
        src_ref=src, dst_ref=dst, send_sem=send, recv_sem=recv, device_id=(row, col), device_id_type=MESH
    )


def meet(devices):
    barrier = pltpu.get_barrier_semaphore()
    for device in devices:
        pl.semaphore_signal(barrier, inc=1, device_id=device, device_id_type=MESH)
    pl.semaphore_wait(barrier, len(devices))


def meet_all(n_row, n_col):
    barrier = pltpu.get_barrier_semaphore()
    me = lax.axis_index("row") * n_col + lax.axis_index("col")
    every = n_row * n_col

    def tell(i, carry):
        to = lax.rem(me + i, every)
        pl.semaphore_signal(barrier, inc=1, device_id=(lax.div(to, n_col), lax.rem(to, n_col)), device_id_type=MESH)
        return carry

    lax.fori_loop(1, every, tell, 0)
    pl.semaphore_wait(barrier, every - 1)


def spread_kernel(n_row, n_col, own_ref, out_ref, land, mine, gather, send1, recv1, send2, recv2):
    r, c = lax.axis_index("row"), lax.axis_index("col")
    meet_all(n_row, n_col)
    sims, panel = own_ref.shape
    part = panel // n_row
    rep = n_row // n_col

    def part_of(row):
        return lax.rem(row, 2) * (n_row // 2) + lax.div(row, 2)

    first = []
    for d in range(1, n_row):
        to = lax.rem(r + d, n_row)
        cp = remote(own_ref.at[:, pl.ds(pl.multiple_of(part_of(to) * part, part), part)], land.at[d - 1],
                    send1.at[d - 1], recv1.at[d - 1], to, c)
        cp.start()
        first.append(cp)
    total = own_ref[:, pl.ds(pl.multiple_of(part_of(r) * part, part), part)].astype(jnp.float32)
    for d in range(1, n_row):
        first[d - 1].wait_recv()
        total = total + land[d - 1].astype(jnp.float32)
    mine[...] = total.astype(mine.dtype)
    sub = lax.rem(part_of(r), rep)
    col_to = lax.div(part_of(r), rep)
    slot = sub * n_col + c
    second = []
    for d in range(n_row):
        to = lax.rem(r + d, n_row)
        cp = remote(mine, gather.at[slot], send2.at[d], recv2.at[slot], to, col_to)
        second.append(cp)
        if d > 0:
            cp.start()
        else:
            @pl.when(col_to != c)
            def _():
                cp.start()

            @pl.when(col_to == c)
            def _():
                gather[slot] = mine[...]
    for s in range(rep):
        for j in range(n_col):
            here = (c * rep + s == part_of(r)) & (c == j)

            @pl.when(jnp.logical_not(here))
            def _():
                remote(mine, gather.at[s * n_col + j], send2.at[0], recv2.at[s * n_col + j], r, c).wait_recv()
    chips = n_col // 2
    core, chip = lax.rem(c, 2), lax.div(c, 2)
    for q in range(n_col):
        other, shift = q // chips, q % chips
        source = lax.rem(chip + shift, chips) * 2 + (core if other == 0 else 1 - core)
        for s in range(rep):
            out_ref[q * sims:(q + 1) * sims, s * part:(s + 1) * part] = gather[s * n_col + source]
    for cp in first:
        cp.wait_send()
    for d in range(n_row):
        if d > 0:
            second[d].wait_send()
        else:
            @pl.when(col_to != c)
            def _():
                second[0].wait_send()


def spread(own, n_row, n_col):
    sims, panel = own.shape
    part = panel // n_row
    vmem = pl.BlockSpec(memory_space=pltpu.VMEM)
    return pl.pallas_call(
        functools.partial(spread_kernel, n_row, n_col),
        out_shape=jax.ShapeDtypeStruct((sims * n_col, panel // n_col), own.dtype),
        in_specs=[vmem],
        out_specs=vmem,
        scratch_shapes=[
            pltpu.VMEM((n_row - 1, sims, part), own.dtype),
            pltpu.VMEM((sims, part), own.dtype),
            pltpu.VMEM((n_row, sims, part), own.dtype),
            pltpu.SemaphoreType.DMA((n_row - 1,)),
            pltpu.SemaphoreType.DMA((n_row - 1,)),
            pltpu.SemaphoreType.DMA((n_row,)),
            pltpu.SemaphoreType.DMA((n_row,)),
        ],
        compiler_params=pltpu.CompilerParams(has_side_effects=True, collective_id=0, vmem_limit_bytes=LIMIT),
        name="spread",
    )(own)


def stream_kernel(n_row, n_col, units, p_ref, apod_ref, obs, prior, proj, out_ref, pout_ref,
                  obs_v, pri_v, proj_v, near_s, near_r, keep, far_s, far_r, w_v, acc, g_s, g_r,
                  swap, fb, yb, gb, zb, hb, xb,
                  os, ps, js, ns, nr, fs, fr, ts, tr, us, ur, gs, gr, s1, r1, s2, r2, s3, r3, s4, r4):
    r, c = lax.axis_index("row"), lax.axis_index("col")
    chips, pairs = n_col // 2, n_row // 2
    core, chip = lax.rem(c, 2), lax.div(c, 2)
    low, high = lax.rem(r, 2), lax.div(r, 2)
    mate, beside = chip * 2 + 1 - core, high * 2 + 1 - low
    sims, rows = out_ref.shape
    prows, slab = proj.shape
    size, half = slab // units, chips * sims

    def other(t, same):
        return lax.rem(chip + t, chips) * 2 + (core if same else 1 - core)

    def span(q, u):
        return pl.ds(pl.multiple_of(q * slab + u * size, size), size)

    def loads(u):
        k, copies = lax.rem(u, IN), []
        for o in range(2):
            for t in range(chips):
                i, at = o * chips + t, span(other(t, o == 1), u)
                copies.append(pltpu.make_async_copy(obs.at[at, :], obs_v.at[k, i], os.at[k, i]))
                copies.append(pltpu.make_async_copy(prior.at[:, at], pri_v.at[k, i], ps.at[k, i]))
        return copies

    def proj_load(u):
        k = lax.rem(u, IN)
        return pltpu.make_async_copy(proj.at[:, pl.ds(pl.multiple_of(u * size, size), size)], proj_v.at[k], js.at[k])

    def near_copy(u):
        k, q = lax.rem(u, near_s.shape[0]), lax.rem(u, near_r.shape[0])
        return remote(near_s.at[k], near_r.at[q], ns.at[k], nr.at[q], r, mate)

    def far_copies(u):
        k, q = lax.rem(u, far_s.shape[0]), lax.rem(u, far_r.shape[0])
        return [remote(far_s.at[k, t - 1], far_r.at[q, t - 1], fs.at[k, t - 1], fr.at[q, t - 1], r, other(t, True))
                for t in range(1, chips)]

    def base_copies(u):
        k = lax.rem(u, keep.shape[0])
        return [remote(keep.at[k, t, half:half + sims], out_ref.at[:, span(other(t, True), u)], ts.at[k, t - 1], tr.at[u, t - 1], r, mate)
                for t in range(1, chips)]

    def base_arrivals(u):
        return [remote(keep.at[0, t, half:half + sims], out_ref.at[:, span(other(t, False), u)], ts.at[0, t - 1], tr.at[u, t - 1], r, mate)
                for t in range(1, chips)]

    def own_copy(u, same=True):
        k = lax.rem(u, keep.shape[0])
        return remote(keep.at[k, 0, half:half + sims], out_ref.at[:, span(other(0, same), u)], us.at[k], ur.at[u], r, mate)

    chunks = 8 if units % 8 == 0 else units
    many = units // chunks

    def back_copies(j):
        at = pl.ds(j * many, many)
        return [remote(g_s.at[(t - 1) * 2 + e, at], g_r.at[(t - 1) * 2 + e, at], gs.at[j, (t - 1) * 2 + e], gr.at[j, (t - 1) * 2 + e], r, other(t, e == 0))
                for t in range(1, chips) for e in range(2)]

    for u in range(min(2, units)):
        for cp in loads(u):
            cp.start()
        proj_load(u).start()
    meet([(r, lax.rem(c + d, n_col)) for d in range(1, n_col)]
         + [(beside, c)] + [(lax.rem(high + d, pairs) * 2 + low, c) for d in range(1, pairs)])
    acc[...] = jnp.zeros_like(acc)

    def sum_chip(u):
        near_copy(u).wait_recv()

        @pl.when(u >= far_s.shape[0])
        def _():
            for cp in far_copies(u - far_s.shape[0]):
                cp.wait_send()

        k, q, e = lax.rem(u, far_s.shape[0]), lax.rem(u, near_r.shape[0]), lax.rem(u, keep.shape[0])
        away, base = far_copies(u), base_copies(u)
        for t in list(range(1, chips)) + [0]:
            lo = keep[e, t, :half] + near_r[q, t, half:]
            hi = keep[e, t, half:] + near_r[q, t, :half]
            if t > 0:
                far_s[k, t - 1, :half] = lo.astype(jnp.bfloat16)
                far_s[k, t - 1, half:] = hi.astype(jnp.bfloat16)
                away[t - 1].start()
                out_ref[:, span(other(t, True), u)] = lo[:sims]
                keep[e, t, half:half + sims] = hi[:sims]
                base[t - 1].start()
            else:
                keep[e, 0, :half] = lo
                keep[e, 0, half:] = hi

    def multiply(u):
        n, k, e = lax.rem(u, IN), lax.rem(u, near_s.shape[0]), lax.rem(u, keep.shape[0])
        for cp in loads(u):
            cp.wait()

        @pl.when(u >= near_s.shape[0])
        def _():
            near_copy(u - near_s.shape[0]).wait_send()

        @pl.when(u >= keep.shape[0])
        def _():
            for cp in base_copies(u - keep.shape[0]) + [own_copy(u - keep.shape[0])]:
                cp.wait_send()

        for o in range(2):
            for t in range(chips):
                value = lax.dot_general(p_ref[...], obs_v[n, o * chips + t], NT, preferred_element_type=jnp.float32)
                first = value[:sims] + pri_v[n, o * chips + t]
                if o == 0:
                    near_s[k, t, :sims] = first
                    near_s[k, t, sims:] = value[sims:]
                else:
                    keep[e, t, :sims] = first
                    keep[e, t, sims:] = value[sims:]
            if o == 0:
                near_copy(u).start()

    def project(u):
        for cp in far_copies(u):
            cp.wait_recv()
        q, e, n = lax.rem(u, far_r.shape[0]), lax.rem(u, keep.shape[0]), lax.rem(u, IN)
        weight = apod_ref[pl.ds(c * units + u, 1), :]
        for h in range(2):
            for b in range(chips):
                at = slice((h * chips + b) * sims, (h * chips + b + 1) * sims)
                total, last = keep[e, 0, at], None
                for t in range(1, chips):
                    s = h * chips + (b + t) % chips
                    term = far_r[q, t - 1, s * sims:(s + 1) * sims].astype(jnp.float32)
                    if b > 0 and t == chips - b:
                        last = term
                    else:
                        total = total + term
                if b > 0:
                    g_s[(b - 1) * 2 + h, u] = total.astype(jnp.bfloat16)
                    total = total + last
                elif h == 0:
                    out_ref[:, span(c, u)] = total
                else:
                    keep[e, 0, half:half + sims] = total
                    own_copy(u).start()
                w_v[at] = (weight * total).astype(jnp.bfloat16)
        proj_load(u).wait()
        tile = min(512, prows)
        for j in range(0, prows, tile):
            acc[:, j:j + tile] += lax.dot_general(w_v[...], proj_v[n, j:j + tile, :], NT, preferred_element_type=jnp.float32)

        @pl.when(u + 2 < units)
        def _():
            proj_load(u + 2).start()

    early = max(0, min((units + D2 - D3) // many, chunks - 1))

    def step(g, carry):
        @pl.when(g + 2 < units)
        def _():
            for cp in loads(g + 2):
                cp.start()

        @pl.when((g >= D2) & (g < units + D2))
        def _():
            sum_chip(g - D2)

        @pl.when(g < units)
        def _():
            multiply(g)

        @pl.when(g >= D3)
        def _():
            project(g - D3)

        @pl.when(g == units + D2 - 1)
        def _():
            for j in range(early):
                for cp in back_copies(j):
                    cp.start()

        return carry

    lax.fori_loop(0, units + D3, step, 0)

    hs, pb = sims // 2, prows // n_row
    pieces = [(t, h) for t in reversed(range(chips)) for h in range(2)]

    def swap_copy(i):
        t, h = pieces[i]
        return remote(acc.at[half + t * sims + h * hs:half + t * sims + (h + 1) * hs], swap.at[i], s1.at[i], r1.at[i], r, mate)

    def y_copy(i):
        return remote(fb.at[i, 1 - low], yb.at[i], s2.at[i], r2.at[i], beside, c)

    def z_copies(i):
        return [remote(gb.at[i, lax.rem(high + d, pairs)], zb.at[i, d - 1], s3.at[i, d - 1], r3.at[i, d - 1], lax.rem(high + d, pairs) * 2 + low, c)
                for d in range(1, pairs)]

    def x_copy(i):
        return remote(hb.at[i], xb.at[i], s4.at[i], r4.at[i], r, other(pieces[i][0], True))

    every = range(len(pieces))
    for i in every:
        swap_copy(i).start()
    for i in every:
        t, h = pieces[i]
        swap_copy(i).wait_recv()
        for k in range(n_row):
            fb[i, k % 2, k // 2] = acc[t * sims + h * hs:t * sims + (h + 1) * hs, k * pb:(k + 1) * pb] + swap[i, :, k * pb:(k + 1) * pb]
        y_copy(i).start()
    for i in every:
        y_copy(i).wait_recv()
        gb[i] = fb[i, low] + yb[i]
        for cp in z_copies(i):
            cp.start()
    for i in every:
        total = gb[i, high]
        for d, cp in enumerate(z_copies(i)):
            cp.wait_recv()
            total = total + zb[i, d]
        hb[i] = total
        if pieces[i][0] > 0:
            x_copy(i).start()
    for j in range(early, chunks):
        for cp in back_copies(j):
            cp.start()

    def finish(j):
        for cp in back_copies(j):
            cp.wait_recv()

        def one(u, carry):
            for cp in base_arrivals(u):
                cp.wait_recv()
            own_copy(u, False).wait_recv()
            for t in range(1, chips):
                for e in range(2):
                    at = span(other(chips - t, e == 0), u)
                    out_ref[:, at] = out_ref[:, at] + g_r[(t - 1) * 2 + e, u].astype(jnp.float32)
            return carry

        lax.fori_loop(j * many, (j + 1) * many, one, 0)

    for j in range(chunks - 1):
        finish(j)
    for h in range(2):
        total = hb[pieces.index((0, h))]
        for t in range(1, chips):
            i = pieces.index((t, h))
            x_copy(i).wait_recv()
            total = total + xb[i]
        pout_ref[h * hs:(h + 1) * hs, :] = total
    finish(chunks - 1)

    for i in every:
        swap_copy(i).wait_send()
        y_copy(i).wait_send()
        for cp in z_copies(i):
            cp.wait_send()
        if pieces[i][0] > 0:
            x_copy(i).wait_send()
    for j in range(chunks):
        for cp in back_copies(j):
            cp.wait_send()
    for b in range(min(units, near_s.shape[0])):
        near_copy(units - 1 - b).wait_send()
    for b in range(min(units, far_s.shape[0])):
        for cp in far_copies(units - 1 - b):
            cp.wait_send()
    for b in range(min(units, keep.shape[0])):
        for cp in base_copies(units - 1 - b) + [own_copy(units - 1 - b)]:
            cp.wait_send()


def stream(picked, obs, prior, apod, proj, n_row, n_col):
    depth, (sims, rows), (prows, slab) = obs.shape[1], prior.shape, proj.shape
    size = math.gcd(slab, UNIT)
    units = slab // size
    chips, pairs = n_col // 2, n_row // 2
    all_sims, pb, hs, pieces = n_col * sims, prows // n_row, sims // 2, 2 * chips
    back = 2 * (chips - 1)
    chunks = 8 if units % 8 == 0 else units
    n_keep, n_far = D3 + 2, 2 * (D3 - D2) + 2
    vmem, anywhere = pl.BlockSpec(memory_space=pltpu.VMEM), pl.BlockSpec(memory_space=pl.ANY)
    dma, bf16, f32 = pltpu.SemaphoreType.DMA, jnp.bfloat16, jnp.float32
    return pl.pallas_call(
        functools.partial(stream_kernel, n_row, n_col, units),
        in_specs=[vmem, vmem, anywhere, anywhere, anywhere],
        out_specs=[vmem, vmem],
        out_shape=[jax.ShapeDtypeStruct((sims, rows), f32), jax.ShapeDtypeStruct((sims, pb), f32)],
        scratch_shapes=[
            pltpu.VMEM((IN, n_col, size, depth), bf16),
            pltpu.VMEM((IN, n_col, sims, size), f32),
            pltpu.VMEM((IN, prows, size), bf16),
            pltpu.VMEM((2, chips, all_sims, size), f32),
            pltpu.VMEM((2 * D2, chips, all_sims, size), f32),
            pltpu.VMEM((n_keep, chips, all_sims, size), f32),
            pltpu.VMEM((SENDS, chips - 1, all_sims, size), bf16),
            pltpu.VMEM((n_far, chips - 1, all_sims, size), bf16),
            pltpu.VMEM((all_sims, size), bf16),
            pltpu.VMEM((all_sims, prows), f32),
            pltpu.VMEM((back, units, sims, size), bf16),
            pltpu.VMEM((back, units, sims, size), bf16),
            pltpu.VMEM((pieces, hs, prows), f32),
            pltpu.VMEM((pieces, 2, pairs, hs, pb), f32),
            pltpu.VMEM((pieces, pairs, hs, pb), f32),
            pltpu.VMEM((pieces, pairs, hs, pb), f32),
            pltpu.VMEM((pieces, pairs - 1, hs, pb), f32),
            pltpu.VMEM((pieces, hs, pb), f32),
            pltpu.VMEM((pieces, hs, pb), f32),
            dma((IN, n_col)), dma((IN, n_col)), dma((IN,)), dma((2,)), dma((2 * D2,)),
            dma((SENDS, chips - 1)), dma((n_far, chips - 1)),
            dma((n_keep, chips - 1)), dma((units, chips - 1)), dma((n_keep,)), dma((units,)),
            dma((chunks, back)), dma((chunks, back)),
            dma((pieces,)), dma((pieces,)), dma((pieces,)), dma((pieces,)),
            dma((pieces, pairs - 1)), dma((pieces, pairs - 1)), dma((pieces,)), dma((pieces,)),
        ],
        compiler_params=pltpu.CompilerParams(has_side_effects=True, collective_id=1, vmem_limit_bytes=LIMIT),
        name="stream",
    )(picked, apod.reshape(n_col * units, size), obs, prior, proj)


def on_device(n_row, n_col, obs_panel, skies, panel_index, prior_sum, apod, proj_panel):
    rows_blk, sims = skies.shape
    local_idx = panel_index - lax.axis_index("row") * rows_blk
    inside = (local_idx >= 0) & (local_idx < rows_blk)
    taken = jnp.take(skies, jnp.clip(local_idx, 0, rows_blk - 1), axis=0)
    own = jnp.where(inside[:, None], taken, jnp.zeros((), jnp.bfloat16)).T
    picked = spread(own, n_row, n_col)
    out, projection = stream(picked, obs_panel, prior_sum.T, apod, proj_panel, n_row, n_col)
    return out.T, projection.T


def solution(mesh):
    in_specs = (P("row", "col"), P("row", "col"), P(), P("row", "col"), P("row"), P(None, ("row", "col")))
    out_specs = (P("row", "col"), P("row", "col"))
    body = functools.partial(on_device, mesh.shape["row"], mesh.shape["col"])
    return jax.shard_map(body, mesh=mesh, in_specs=in_specs, out_specs=out_specs, check_vma=False)
```

```python
import functools
import math

import jax
import jax.numpy as jnp
from jax import lax
from jax.experimental import pallas as pl
from jax.experimental.pallas import tpu as pltpu
from jax.sharding import PartitionSpec as P

MESH = pl.DeviceIdType.MESH
NT = (((1,), (1,)), ((), ()))
UNIT = 256
D2, D3 = 1, 4
IN, SENDS = 3, 3
LIMIT = 46 * 1024 * 1024
LANES = 128


def remote(src, dst, send, recv, row, col):
    return pltpu.make_async_remote_copy(
        src_ref=src, dst_ref=dst, send_sem=send, recv_sem=recv, device_id=(row, col), device_id_type=MESH
    )


def greet(n_row, n_col):
    me, every = lax.axis_index("row") * n_col + lax.axis_index("col"), n_row * n_col

    def tell(i, carry):
        to = lax.rem(me + i, every)
        pl.semaphore_signal(pltpu.get_barrier_semaphore(), inc=1, device_id=(lax.div(to, n_col), lax.rem(to, n_col)), device_id_type=MESH)
        return carry

    lax.fori_loop(1, every, tell, 0)


def tabulate(r, idx_ref, held, table, where_v, where_s, loads, where_sem):
    groups, sims, width = held.shape
    rows, lanes = groups * width, table.shape[1]
    parts = lanes // sims
    span = width // parts
    at = idx_ref[...] - r * rows
    near = jnp.clip(at, 0, rows - 1)
    where_v[...] = lax.div(near, width) * span + lax.rem(near, span)
    codes = pltpu.make_async_copy(where_v, where_s, where_sem)
    codes.start()
    one = (lax.broadcasted_iota(jnp.int32, (span, span), 0) == lax.broadcasted_iota(jnp.int32, (span, span), 1)).astype(held.dtype)
    batch = max(1, groups // 4)
    for first in range(0, groups, batch):
        some = range(first, min(groups, first + batch))
        for g in some:
            loads[g].wait()
        for g in some:
            block = jnp.concatenate([held[g, :, b * span:(b + 1) * span] for b in range(parts)], axis=0)
            table[g * span:(g + 1) * span, :] = lax.dot_general(one, block, NT, preferred_element_type=jnp.float32)
    codes.wait()
    where_v[...] = jnp.where((at >= 0) & (at < rows), lax.rem(lax.div(near, span), parts), -1)


def spread(n_row, n_col, r, c, p_ref, table, where_v, where_s, rows_v, own, land, mine, gather, send1, recv1, send2, recv2):
    halves, sims, part = own.shape[1], own.shape[1] * own.shape[2], own.shape[3]
    hs, lanes, rep = sims // halves, table.shape[1], n_row // n_col
    tiles = part // LANES
    turn = (lax.broadcasted_iota(jnp.int32, (lanes, lanes), 0) == lax.broadcasted_iota(jnp.int32, (lanes, lanes), 1)).astype(own.dtype)

    def part_of(row):
        return lax.rem(row, 2) * (n_row // 2) + lax.div(row, 2)

    def first_copy(d, h):
        to = lax.rem(r + d, n_row)
        return remote(own.at[part_of(to), h], land.at[h, d - 1], send1.at[h, d - 1], recv1.at[h, d - 1], to, c)

    def collect(i, carry):
        d = lax.rem(i + 1, n_row)
        k = part_of(lax.rem(r + d, n_row))
        for t in range(tiles):
            for j in range(LANES):
                rows_v[t * LANES + j:t * LANES + j + 1, :] = table[pl.ds(where_s[k * tiles + t, j], 1), :]
        for t in range(tiles):
            flat = lax.dot_general(turn, rows_v[t * LANES:(t + 1) * LANES, :].astype(own.dtype), NT, preferred_element_type=jnp.float32)
            which = where_v[pl.ds(k * tiles + t, 1), :]
            total = jnp.zeros((sims, LANES), jnp.float32)
            for b in range(lanes // sims):
                total = jnp.where(which == b, flat[b * sims:(b + 1) * sims], total)
            for h in range(halves):
                own[k, h, :, t * LANES:(t + 1) * LANES] = total[h * hs:(h + 1) * hs].astype(own.dtype)

        @pl.when(d > 0)
        def _():
            for h in range(halves):
                first_copy(d, h).start()

        return carry

    lax.fori_loop(0, n_row, collect, 0)
    sub, col_to = lax.rem(part_of(r), rep), lax.div(part_of(r), rep)
    slot = sub * n_col + c

    def second_copy(d, h):
        return remote(mine.at[h], gather.at[slot, h], send2.at[h, d], recv2.at[h, slot], lax.rem(r + d, n_row), col_to)

    for h in range(halves):
        total = own[part_of(r), h].astype(jnp.float32)
        for d in range(1, n_row):
            first_copy(d, h).wait_recv()
            total = total + land[h, d - 1].astype(jnp.float32)
        mine[h] = total.astype(mine.dtype)
        for d in range(1, n_row):
            second_copy(d, h).start()

        @pl.when(col_to != c)
        def _():
            second_copy(0, h).start()

        @pl.when(col_to == c)
        def _():
            gather[slot, h] = mine[h]

    chips = n_col // 2
    core, chip = lax.rem(c, 2), lax.div(c, 2)
    for h in range(halves):
        for s in range(rep):
            for j in range(n_col):
                @pl.when(jnp.logical_not((c * rep + s == part_of(r)) & (c == j)))
                def _():
                    remote(mine.at[h], gather.at[s * n_col + j, h], send2.at[h, 0], recv2.at[h, s * n_col + j], r, c).wait_recv()
        for q in range(n_col):
            source = lax.rem(chip + q % chips, chips) * 2 + (core if q // chips == 0 else 1 - core)
            for s in range(rep):
                p_ref[q * sims + h * hs:q * sims + (h + 1) * hs, s * part:(s + 1) * part] = gather[s * n_col + source, h]

    def drain():
        for h in range(halves):
            for d in range(1, n_row):
                first_copy(d, h).wait_send()
                second_copy(d, h).wait_send()

            @pl.when(col_to != c)
            def _():
                second_copy(0, h).wait_send()

    return drain


def stream_kernel(n_row, n_col, units, idx_ref, maps, apod, obs, prior, proj, out_ref, pout_ref,
                  held, table, where_v, where_s, rows_v, own, land, mine, gather, p_ref,
                  apod_ref, obs_v, pri_v, proj_v, near_s, near_r, keep, far_s, far_r, w_v, acc, g_s, g_r,
                  swap, fb, yb, gb, zb, hb, xb,
                  ms, ws, s5, r5, s6, r6, aps, os, ps, js, ns, nr, fs, fr, ts, tr, us, ur, gs, gr, s1, r1, s2, r2, s3, r3, s4, r4):
    r, c = lax.axis_index("row"), lax.axis_index("col")
    chips, pairs = n_col // 2, n_row // 2
    core, chip = lax.rem(c, 2), lax.div(c, 2)
    low, high = lax.rem(r, 2), lax.div(r, 2)
    mate, beside = chip * 2 + 1 - core, high * 2 + 1 - low
    sims, rows = out_ref.shape
    prows, slab = proj.shape
    size, half = slab // units, chips * sims

    def other(t, same):
        return lax.rem(chip + t, chips) * 2 + (core if same else 1 - core)

    def span(q, u):
        return pl.ds(pl.multiple_of(q * slab + u * size, size), size)

    def loads(u):
        k, copies = lax.rem(u, IN), []
        for o in range(2):
            for t in range(chips):
                i, at = o * chips + t, span(other(t, o == 1), u)
                copies.append(pltpu.make_async_copy(obs.at[at, :], obs_v.at[k, i], os.at[k, i]))
                copies.append(pltpu.make_async_copy(prior.at[:, at], pri_v.at[k, i], ps.at[k, i]))
        return copies

    def proj_load(u):
        k = lax.rem(u, IN)
        return pltpu.make_async_copy(proj.at[:, pl.ds(pl.multiple_of(u * size, size), size)], proj_v.at[k], js.at[k])

    def near_copy(u):
        k, q = lax.rem(u, near_s.shape[0]), lax.rem(u, near_r.shape[0])
        return remote(near_s.at[k], near_r.at[q], ns.at[k], nr.at[q], r, mate)

    def far_copies(u):
        k, q = lax.rem(u, far_s.shape[0]), lax.rem(u, far_r.shape[0])
        return [remote(far_s.at[k, t - 1], far_r.at[q, t - 1], fs.at[k, t - 1], fr.at[q, t - 1], r, other(t, True))
                for t in range(1, chips)]

    def base_copies(u):
        k = lax.rem(u, keep.shape[0])
        return [remote(keep.at[k, t, half:half + sims], out_ref.at[:, span(other(t, True), u)], ts.at[k, t - 1], tr.at[u, t - 1], r, mate)
                for t in range(1, chips)]

    def base_arrivals(u):
        return [remote(keep.at[0, t, half:half + sims], out_ref.at[:, span(other(t, False), u)], ts.at[0, t - 1], tr.at[u, t - 1], r, mate)
                for t in range(1, chips)]

    def own_copy(u, same=True):
        k = lax.rem(u, keep.shape[0])
        return remote(keep.at[k, 0, half:half + sims], out_ref.at[:, span(other(0, same), u)], us.at[k], ur.at[u], r, mate)

    chunks = 8 if units % 8 == 0 else units
    many = units // chunks

    def back_copies(j):
        at = pl.ds(j * many, many)
        return [remote(g_s.at[(t - 1) * 2 + e, at], g_r.at[(t - 1) * 2 + e, at], gs.at[j, (t - 1) * 2 + e], gr.at[j, (t - 1) * 2 + e], r, other(t, e == 0))
                for t in range(1, chips) for e in range(2)]

    width = held.shape[2]
    tables = [pltpu.make_async_copy(maps.at[:, g * width:(g + 1) * width], held.at[g], ms.at[g]) for g in range(held.shape[0])]
    weights = pltpu.make_async_copy(apod, apod_ref, aps)
    for cp in tables + [weights]:
        cp.start()
    for u in range(min(2, units)):
        for cp in loads(u):
            cp.start()
        proj_load(u).start()
    greet(n_row, n_col)
    acc[...] = jnp.zeros_like(acc)
    tabulate(r, idx_ref, held, table, where_v, where_s, tables, ws)
    pl.semaphore_wait(pltpu.get_barrier_semaphore(), n_row * n_col - 1)
    drain = spread(n_row, n_col, r, c, p_ref, table, where_v, where_s, rows_v, own, land, mine, gather, s5, r5, s6, r6)
    weights.wait()

    def sum_chip(u):
        near_copy(u).wait_recv()

        @pl.when(u >= far_s.shape[0])
        def _():
            for cp in far_copies(u - far_s.shape[0]):
                cp.wait_send()

        k, q, e = lax.rem(u, far_s.shape[0]), lax.rem(u, near_r.shape[0]), lax.rem(u, keep.shape[0])
        away, base = far_copies(u), base_copies(u)
        for t in list(range(1, chips)) + [0]:
            lo = keep[e, t, :half] + near_r[q, t, half:]
            hi = keep[e, t, half:] + near_r[q, t, :half]
            if t > 0:
                far_s[k, t - 1, :half] = lo.astype(jnp.bfloat16)
                far_s[k, t - 1, half:] = hi.astype(jnp.bfloat16)
                away[t - 1].start()
                out_ref[:, span(other(t, True), u)] = lo[:sims]
                keep[e, t, half:half + sims] = hi[:sims]
                base[t - 1].start()
            else:
                keep[e, 0, :half] = lo
                keep[e, 0, half:] = hi

    def multiply(u):
        n, k, e = lax.rem(u, IN), lax.rem(u, near_s.shape[0]), lax.rem(u, keep.shape[0])
        for cp in loads(u):
            cp.wait()

        @pl.when(u >= near_s.shape[0])
        def _():
            near_copy(u - near_s.shape[0]).wait_send()

        @pl.when(u >= keep.shape[0])
        def _():
            for cp in base_copies(u - keep.shape[0]) + [own_copy(u - keep.shape[0])]:
                cp.wait_send()

        for o in range(2):
            for t in range(chips):
                value = lax.dot_general(p_ref[...], obs_v[n, o * chips + t], NT, preferred_element_type=jnp.float32)
                first = value[:sims] + pri_v[n, o * chips + t]
                if o == 0:
                    near_s[k, t, :sims] = first
                    near_s[k, t, sims:] = value[sims:]
                else:
                    keep[e, t, :sims] = first
                    keep[e, t, sims:] = value[sims:]
            if o == 0:
                near_copy(u).start()

    def project(u):
        for cp in far_copies(u):
            cp.wait_recv()
        q, e, n = lax.rem(u, far_r.shape[0]), lax.rem(u, keep.shape[0]), lax.rem(u, IN)
        wide = size // LANES
        weight = jnp.concatenate([apod_ref[pl.ds((c * units + u) * wide + i, 1), :] for i in range(wide)], axis=1)
        for h in range(2):
            for b in range(chips):
                at = slice((h * chips + b) * sims, (h * chips + b + 1) * sims)
                total, last = keep[e, 0, at], None
                for t in range(1, chips):
                    s = h * chips + (b + t) % chips
                    term = far_r[q, t - 1, s * sims:(s + 1) * sims].astype(jnp.float32)
                    if b > 0 and t == chips - b:
                        last = term
                    else:
                        total = total + term
                if b > 0:
                    g_s[(b - 1) * 2 + h, u] = total.astype(jnp.bfloat16)
                    total = total + last
                elif h == 0:
                    out_ref[:, span(c, u)] = total
                else:
                    keep[e, 0, half:half + sims] = total
                    own_copy(u).start()
                w_v[at] = (weight * total).astype(jnp.bfloat16)
        proj_load(u).wait()
        tile = min(512, prows)
        for j in range(0, prows, tile):
            acc[:, j:j + tile] += lax.dot_general(w_v[...], proj_v[n, j:j + tile, :], NT, preferred_element_type=jnp.float32)

        @pl.when(u + 2 < units)
        def _():
            proj_load(u + 2).start()

    early = max(0, min((units + D2 - D3) // many, chunks - 1))

    def step(g, carry):
        @pl.when(g + 2 < units)
        def _():
            for cp in loads(g + 2):
                cp.start()

        @pl.when((g >= D2) & (g < units + D2))
        def _():
            sum_chip(g - D2)

        @pl.when(g < units)
        def _():
            multiply(g)

        @pl.when(g >= D3)
        def _():
            project(g - D3)

        @pl.when(g == units + D2 - 1)
        def _():
            for j in range(early):
                for cp in back_copies(j):
                    cp.start()

        return carry

    lax.fori_loop(0, units + D3, step, 0)

    hs, pb = sims // 2, prows // n_row
    pieces = [(t, h) for t in reversed(range(chips)) for h in range(2)]

    def swap_copy(i):
        t, h = pieces[i]
        return remote(acc.at[half + t * sims + h * hs:half + t * sims + (h + 1) * hs], swap.at[i], s1.at[i], r1.at[i], r, mate)

    def y_copy(i):
        return remote(fb.at[i, 1 - low], yb.at[i], s2.at[i], r2.at[i], beside, c)

    def z_copies(i):
        return [remote(gb.at[i, lax.rem(high + d, pairs)], zb.at[i, d - 1], s3.at[i, d - 1], r3.at[i, d - 1], lax.rem(high + d, pairs) * 2 + low, c)
                for d in range(1, pairs)]

    def x_copy(i):
        return remote(hb.at[i], xb.at[i], s4.at[i], r4.at[i], r, other(pieces[i][0], True))

    every = range(len(pieces))
    for i in every:
        swap_copy(i).start()
    for i in every:
        t, h = pieces[i]
        swap_copy(i).wait_recv()
        for k in range(n_row):
            fb[i, k % 2, k // 2] = acc[t * sims + h * hs:t * sims + (h + 1) * hs, k * pb:(k + 1) * pb] + swap[i, :, k * pb:(k + 1) * pb]
        y_copy(i).start()
    for i in every:
        y_copy(i).wait_recv()
        gb[i] = fb[i, low] + yb[i]
        for cp in z_copies(i):
            cp.start()
    for i in every:
        total = gb[i, high]
        for d, cp in enumerate(z_copies(i)):
            cp.wait_recv()
            total = total + zb[i, d]
        hb[i] = total
        if pieces[i][0] > 0:
            x_copy(i).start()
    for j in range(early, chunks):
        for cp in back_copies(j):
            cp.start()

    def finish(j):
        for cp in back_copies(j):
            cp.wait_recv()

        def one(u, carry):
            for cp in base_arrivals(u):
                cp.wait_recv()
            own_copy(u, False).wait_recv()
            for t in range(1, chips):
                for e in range(2):
                    at = span(other(chips - t, e == 0), u)
                    out_ref[:, at] = out_ref[:, at] + g_r[(t - 1) * 2 + e, u].astype(jnp.float32)
            return carry

        lax.fori_loop(j * many, (j + 1) * many, one, 0)

    for j in range(chunks - 1):
        finish(j)
    for h in range(2):
        total = hb[pieces.index((0, h))]
        for t in range(1, chips):
            i = pieces.index((t, h))
            x_copy(i).wait_recv()
            total = total + xb[i]
        pout_ref[h * hs:(h + 1) * hs, :] = total
    finish(chunks - 1)

    drain()
    for i in every:
        swap_copy(i).wait_send()
        y_copy(i).wait_send()
        for cp in z_copies(i):
            cp.wait_send()
        if pieces[i][0] > 0:
            x_copy(i).wait_send()
    for j in range(chunks):
        for cp in back_copies(j):
            cp.wait_send()
    for b in range(min(units, near_s.shape[0])):
        near_copy(units - 1 - b).wait_send()
    for b in range(min(units, far_s.shape[0])):
        for cp in far_copies(units - 1 - b):
            cp.wait_send()
    for b in range(min(units, keep.shape[0])):
        for cp in base_copies(units - 1 - b) + [own_copy(units - 1 - b)]:
            cp.wait_send()


def stream(index, maps, obs, prior, apod, proj, n_row, n_col):
    depth, (sims, rows), (prows, slab) = obs.shape[1], prior.shape, proj.shape
    panel, part = index.shape[0], index.shape[0] // n_row
    parts = max(1, LANES // sims)
    width = parts * math.gcd(UNIT, rows // parts)
    halves = 2
    size = math.gcd(slab, UNIT)
    units = slab // size
    chips, pairs = n_col // 2, n_row // 2
    all_sims, pb, hs, pieces = n_col * sims, prows // n_row, sims // 2, 2 * chips
    back = 2 * (chips - 1)
    chunks = 8 if units % 8 == 0 else units
    n_keep, n_far = D3 + 2, 2 * (D3 - D2) + 2
    vmem, anywhere = pl.BlockSpec(memory_space=pltpu.VMEM), pl.BlockSpec(memory_space=pltpu.HBM)
    dma, bf16, f32 = pltpu.SemaphoreType.DMA, jnp.bfloat16, jnp.float32
    return pl.pallas_call(
        functools.partial(stream_kernel, n_row, n_col, units),
        in_specs=[vmem] + [anywhere] * 5,
        out_specs=[vmem, vmem],
        out_shape=[jax.ShapeDtypeStruct((sims, rows), f32), jax.ShapeDtypeStruct((sims, pb), f32)],
        scratch_shapes=[
            pltpu.VMEM((rows // width, sims, width), bf16),
            pltpu.VMEM((rows // parts, parts * sims), f32),
            pltpu.VMEM((panel // LANES, LANES), jnp.int32),
            pltpu.SMEM((panel // LANES, LANES), jnp.int32),
            pltpu.VMEM((part, parts * sims), f32),
            pltpu.VMEM((n_row, halves, sims // halves, part), bf16),
            pltpu.VMEM((halves, n_row - 1, sims // halves, part), bf16),
            pltpu.VMEM((halves, sims // halves, part), bf16),
            pltpu.VMEM((n_row, halves, sims // halves, part), bf16),
            pltpu.VMEM((all_sims, depth), bf16),
            pltpu.VMEM((rows // LANES, LANES), f32),
            pltpu.VMEM((IN, n_col, size, depth), bf16),
            pltpu.VMEM((IN, n_col, sims, size), f32),
            pltpu.VMEM((IN, prows, size), bf16),
            pltpu.VMEM((2, chips, all_sims, size), f32),
            pltpu.VMEM((2 * D2, chips, all_sims, size), f32),
            pltpu.VMEM((n_keep, chips, all_sims, size), f32),
            pltpu.VMEM((SENDS, chips - 1, all_sims, size), bf16),
            pltpu.VMEM((n_far, chips - 1, all_sims, size), bf16),
            pltpu.VMEM((all_sims, size), bf16),
            pltpu.VMEM((all_sims, prows), f32),
            pltpu.VMEM((back, units, sims, size), bf16),
            pltpu.VMEM((back, units, sims, size), bf16),
            pltpu.VMEM((pieces, hs, prows), f32),
            pltpu.VMEM((pieces, 2, pairs, hs, pb), f32),
            pltpu.VMEM((pieces, pairs, hs, pb), f32),
            pltpu.VMEM((pieces, pairs, hs, pb), f32),
            pltpu.VMEM((pieces, pairs - 1, hs, pb), f32),
            pltpu.VMEM((pieces, hs, pb), f32),
            pltpu.VMEM((pieces, hs, pb), f32),
            dma((rows // width,)), dma, dma((halves, n_row - 1)), dma((halves, n_row - 1)), dma((halves, n_row)), dma((halves, n_row)),
            dma, dma((IN, n_col)), dma((IN, n_col)), dma((IN,)), dma((2,)), dma((2 * D2,)),
            dma((SENDS, chips - 1)), dma((n_far, chips - 1)),
            dma((n_keep, chips - 1)), dma((units, chips - 1)), dma((n_keep,)), dma((units,)),
            dma((chunks, back)), dma((chunks, back)),
            dma((pieces,)), dma((pieces,)), dma((pieces,)), dma((pieces,)),
            dma((pieces, pairs - 1)), dma((pieces, pairs - 1)), dma((pieces,)), dma((pieces,)),
        ],
        compiler_params=pltpu.CompilerParams(has_side_effects=True, collective_id=0, vmem_limit_bytes=LIMIT),
        name="stream",
    )(index.reshape(panel // LANES, LANES), *[pltpu.with_memory_space_constraint(x, pltpu.HBM) for x in (maps, apod.reshape(rows // LANES, LANES), obs, prior, proj)])


def on_device(n_row, n_col, obs_panel, skies, panel_index, prior_sum, apod, proj_panel):
    out, projection = stream(panel_index, skies.T, obs_panel, prior_sum.T, apod, proj_panel, n_row, n_col)
    return out.T, projection.T


def solution(mesh):
    in_specs = (P("row", "col"), P("row", "col"), P(), P("row", "col"), P("row"), P(None, ("row", "col")))
    out_specs = (P("row", "col"), P("row", "col"))
    body = functools.partial(on_device, mesh.shape["row"], mesh.shape["col"])
    return jax.shard_map(body, mesh=mesh, in_specs=in_specs, out_specs=out_specs, check_vma=False)
```

```python
import functools
import math

import jax
import jax.numpy as jnp
from jax import lax
from jax.experimental import pallas as pl
from jax.experimental.pallas import tpu as pltpu
from jax.sharding import PartitionSpec as P

MESH = pl.DeviceIdType.MESH
NT = (((1,), (1,)), ((), ()))
UNIT = 256
D2, D3 = 1, 4
IN, SENDS = 3, 3
LIMIT = 46 * 1024 * 1024
LANES = 128
AHEAD = 3


def remote(src, dst, send, recv, row, col):
    return pltpu.make_async_remote_copy(
        src_ref=src, dst_ref=dst, send_sem=send, recv_sem=recv, device_id=(row, col), device_id_type=MESH
    )


def greet(devices):
    for device in devices:
        pl.semaphore_signal(pltpu.get_barrier_semaphore(), inc=1, device_id=device, device_id_type=MESH)


def tabulate(r, idx_ref, held, table, where_v, where_s, loads, where_sem):
    groups, sims, width = held.shape
    rows, lanes = groups * width, table.shape[1]
    parts = lanes // sims
    span = width // parts
    at = idx_ref[...] - r * rows
    near = jnp.clip(at, 0, rows - 1)
    where_v[...] = lax.div(near, width) * span + lax.rem(near, span)
    codes = pltpu.make_async_copy(where_v, where_s, where_sem)
    codes.start()
    one = (lax.broadcasted_iota(jnp.int32, (span, span), 0) == lax.broadcasted_iota(jnp.int32, (span, span), 1)).astype(held.dtype)
    pair = 2 if groups % 2 == 0 else 1
    batch = max(1, groups // pair // 4) * pair
    for first in range(0, groups, batch):
        some = range(first, min(groups, first + batch))
        for g in some:
            loads[g].wait()
        for g in some[::pair]:
            block = jnp.concatenate([held[i, :, b * span:(b + 1) * span] for i in range(g, g + pair) for b in range(parts)], axis=0)
            turned = lax.dot_general(one, block, NT, preferred_element_type=jnp.float32)
            for i in range(pair):
                table[(g + i) * span:(g + i + 1) * span, :] = turned[:, i * lanes:(i + 1) * lanes]
    codes.wait()
    where_v[...] = jnp.where((at >= 0) & (at < rows), lax.rem(lax.div(near, span), parts), -1)


def spread(n_row, n_col, r, c, peers, ready, p_ref, table, where_v, where_s, rows_v, own, land, mine, gather, send1, recv1, send2, recv2):
    halves, sims, part = own.shape[1], own.shape[1] * own.shape[2], own.shape[3]
    hs, lanes, rep = sims // halves, table.shape[1], n_row // n_col
    tiles = part // LANES
    turn = (lax.broadcasted_iota(jnp.int32, (lanes, lanes), 0) == lax.broadcasted_iota(jnp.int32, (lanes, lanes), 1)).astype(own.dtype)

    def part_of(row):
        return lax.rem(row, 2) * (n_row // 2) + lax.div(row, 2)

    def first_copy(d, h):
        to = lax.rem(r + d, n_row)
        return remote(own.at[part_of(to), h], land.at[h, d - 1], send1.at[h, d - 1], recv1.at[h, d - 1], to, c)

    def collect(i, carry):
        d = lax.rem(i + 1, n_row)
        k = part_of(lax.rem(r + d, n_row))
        for t in range(tiles):
            for j in range(LANES):
                rows_v[t * LANES + j:t * LANES + j + 1, :] = table[pl.ds(where_s[k * tiles + t, j], 1), :]
        for t in range(tiles):
            flat = lax.dot_general(turn, rows_v[t * LANES:(t + 1) * LANES, :].astype(own.dtype), NT, preferred_element_type=jnp.float32)
            which = where_v[pl.ds(k * tiles + t, 1), :]
            total = jnp.zeros((sims, LANES), jnp.float32)
            for b in range(lanes // sims):
                total = jnp.where(which == b, flat[b * sims:(b + 1) * sims], total)
            for h in range(halves):
                own[k, h, :, t * LANES:(t + 1) * LANES] = total[h * hs:(h + 1) * hs].astype(own.dtype)

        return d

    def collect_and_send(i, carry):
        d = collect(i, carry)

        @pl.when(d > 0)
        def _():
            for h in range(halves):
                first_copy(d, h).start()

        return carry

    ahead = min(AHEAD, n_row - 1)
    lax.fori_loop(0, ahead, lambda i, carry: (collect(i, carry), carry)[1], 0)
    pl.semaphore_wait(pltpu.get_barrier_semaphore(), n_row + n_col - 2)
    for device in peers:
        pl.semaphore_signal(ready, inc=1, device_id=device, device_id_type=MESH)
    for d in range(1, ahead + 1):
        for h in range(halves):
            first_copy(d, h).start()
    lax.fori_loop(ahead, n_row, collect_and_send, 0)
    pl.semaphore_wait(ready, n_col - 1)
    sub, col_to = lax.rem(part_of(r), rep), lax.div(part_of(r), rep)
    slot = sub * n_col + c

    def second_copy(d, h):
        return remote(mine.at[h], gather.at[slot, h], send2.at[h, d], recv2.at[h, slot], lax.rem(r + d, n_row), col_to)

    for h in range(halves):
        total = own[part_of(r), h].astype(jnp.float32)
        for d in range(1, n_row):
            first_copy(d, h).wait_recv()
            total = total + land[h, d - 1].astype(jnp.float32)
        mine[h] = total.astype(mine.dtype)
        for d in range(1, n_row):
            second_copy(d, h).start()

        @pl.when(col_to != c)
        def _():
            second_copy(0, h).start()

        @pl.when(col_to == c)
        def _():
            gather[slot, h] = mine[h]

    chips = n_col // 2
    core, chip = lax.rem(c, 2), lax.div(c, 2)
    for h in range(halves):
        for s in range(rep):
            for j in range(n_col):
                @pl.when(jnp.logical_not((c * rep + s == part_of(r)) & (c == j)))
                def _():
                    remote(mine.at[h], gather.at[s * n_col + j, h], send2.at[h, 0], recv2.at[h, s * n_col + j], r, c).wait_recv()
        for q in range(n_col):
            source = lax.rem(chip + q % chips, chips) * 2 + (core if q // chips == 0 else 1 - core)
            for s in range(rep):
                p_ref[q * sims + h * hs:q * sims + (h + 1) * hs, s * part:(s + 1) * part] = gather[s * n_col + source, h]

    def drain():
        for h in range(halves):
            for d in range(1, n_row):
                first_copy(d, h).wait_send()
                second_copy(d, h).wait_send()

            @pl.when(col_to != c)
            def _():
                second_copy(0, h).wait_send()

    return drain


def stream_kernel(n_row, n_col, units, idx_ref, maps, apod, obs, prior, proj, out_ref, pout_ref,
                  held, table, where_v, where_s, rows_v, own, land, mine, gather, p_ref,
                  apod_ref, obs_v, pri_v, proj_v, near_s, near_r, keep, far_s, far_r, w_v, acc, g_s, g_r,
                  swap, fb, yb, gb, zb, hb, xb,
                  ready, ms, ws, s5, r5, s6, r6, aps, os, ps, js, ns, nr, fs, fr, ts, tr, us, ur, gs, gr, s1, r1, s2, r2, s3, r3, s4, r4):
    r, c = lax.axis_index("row"), lax.axis_index("col")
    chips, pairs = n_col // 2, n_row // 2
    core, chip = lax.rem(c, 2), lax.div(c, 2)
    low, high = lax.rem(r, 2), lax.div(r, 2)
    mate, beside = chip * 2 + 1 - core, high * 2 + 1 - low
    sims, rows = out_ref.shape
    prows, slab = proj.shape
    size, half = slab // units, chips * sims

    def other(t, same):
        return lax.rem(chip + t, chips) * 2 + (core if same else 1 - core)

    def span(q, u):
        return pl.ds(pl.multiple_of(q * slab + u * size, size), size)

    def loads(u):
        k, copies = lax.rem(u, IN), []
        for o in range(2):
            for t in range(chips):
                i, at = o * chips + t, span(other(t, o == 1), u)
                copies.append(pltpu.make_async_copy(obs.at[at, :], obs_v.at[k, i], os.at[k, i]))
                copies.append(pltpu.make_async_copy(prior.at[:, at], pri_v.at[k, i], ps.at[k, i]))
        return copies

    def proj_load(u):
        k = lax.rem(u, IN)
        return pltpu.make_async_copy(proj.at[:, pl.ds(pl.multiple_of(u * size, size), size)], proj_v.at[k], js.at[k])

    def near_copy(u):
        k, q = lax.rem(u, near_s.shape[0]), lax.rem(u, near_r.shape[0])
        return remote(near_s.at[k], near_r.at[q], ns.at[k], nr.at[q], r, mate)

    def far_copies(u):
        k, q = lax.rem(u, far_s.shape[0]), lax.rem(u, far_r.shape[0])
        return [remote(far_s.at[k, t - 1], far_r.at[q, t - 1], fs.at[k, t - 1], fr.at[q, t - 1], r, other(t, True))
                for t in range(1, chips)]

    def base_copies(u):
        k = lax.rem(u, keep.shape[0])
        return [remote(keep.at[k, t, half:half + sims], out_ref.at[:, span(other(t, True), u)], ts.at[k, t - 1], tr.at[u, t - 1], r, mate)
                for t in range(1, chips)]

    def base_arrivals(u):
        return [remote(keep.at[0, t, half:half + sims], out_ref.at[:, span(other(t, False), u)], ts.at[0, t - 1], tr.at[u, t - 1], r, mate)
                for t in range(1, chips)]

    def own_copy(u, same=True):
        k = lax.rem(u, keep.shape[0])
        return remote(keep.at[k, 0, half:half + sims], out_ref.at[:, span(other(0, same), u)], us.at[k], ur.at[u], r, mate)

    chunks = 8 if units % 8 == 0 else units
    many = units // chunks

    def back_copies(j):
        at = pl.ds(j * many, many)
        return [remote(g_s.at[(t - 1) * 2 + e, at], g_r.at[(t - 1) * 2 + e, at], gs.at[j, (t - 1) * 2 + e], gr.at[j, (t - 1) * 2 + e], r, other(t, e == 0))
                for t in range(1, chips) for e in range(2)]

    width = held.shape[2]
    tables = [pltpu.make_async_copy(maps.at[:, g * width:(g + 1) * width], held.at[g], ms.at[g]) for g in range(held.shape[0])]
    weights = pltpu.make_async_copy(apod, apod_ref, aps)
    for cp in tables:
        cp.start()
    line, peers = [(lax.rem(r + d, n_row), c) for d in range(1, n_row)], [(r, lax.rem(c + d, n_col)) for d in range(1, n_col)]
    greet(line + peers)
    acc[...] = jnp.zeros_like(acc)
    tabulate(r, idx_ref, held, table, where_v, where_s, tables, ws)
    for cp in [weights] + [cp for u in range(min(2, units)) for cp in loads(u) + [proj_load(u)]]:
        cp.start()
    drain = spread(n_row, n_col, r, c, peers, ready, p_ref, table, where_v, where_s, rows_v, own, land, mine, gather, s5, r5, s6, r6)
    weights.wait()

    def sum_chip(u):
        near_copy(u).wait_recv()

        @pl.when(u >= far_s.shape[0])
        def _():
            for cp in far_copies(u - far_s.shape[0]):
                cp.wait_send()

        k, q, e = lax.rem(u, far_s.shape[0]), lax.rem(u, near_r.shape[0]), lax.rem(u, keep.shape[0])
        away, base = far_copies(u), base_copies(u)
        for t in list(range(1, chips)) + [0]:
            lo = keep[e, t, :half] + near_r[q, t, half:]
            hi = keep[e, t, half:] + near_r[q, t, :half]
            if t > 0:
                far_s[k, t - 1, :half] = lo.astype(jnp.bfloat16)
                far_s[k, t - 1, half:] = hi.astype(jnp.bfloat16)
                away[t - 1].start()
                out_ref[:, span(other(t, True), u)] = lo[:sims]
                keep[e, t, half:half + sims] = hi[:sims]
                base[t - 1].start()
            else:
                keep[e, 0, :half] = lo
                keep[e, 0, half:] = hi

    def multiply(u):
        n, k, e = lax.rem(u, IN), lax.rem(u, near_s.shape[0]), lax.rem(u, keep.shape[0])
        for cp in loads(u):
            cp.wait()

        @pl.when(u >= near_s.shape[0])
        def _():
            near_copy(u - near_s.shape[0]).wait_send()

        @pl.when(u >= keep.shape[0])
        def _():
            for cp in base_copies(u - keep.shape[0]) + [own_copy(u - keep.shape[0])]:
                cp.wait_send()

        for o in range(2):
            for t in range(chips):
                value = lax.dot_general(p_ref[...], obs_v[n, o * chips + t], NT, preferred_element_type=jnp.float32)
                first = value[:sims] + pri_v[n, o * chips + t]
                if o == 0:
                    near_s[k, t, :sims] = first
                    near_s[k, t, sims:] = value[sims:]
                else:
                    keep[e, t, :sims] = first
                    keep[e, t, sims:] = value[sims:]
            if o == 0:
                near_copy(u).start()

    def project(u):
        for cp in far_copies(u):
            cp.wait_recv()
        q, e, n = lax.rem(u, far_r.shape[0]), lax.rem(u, keep.shape[0]), lax.rem(u, IN)
        wide = size // LANES
        weight = jnp.concatenate([apod_ref[pl.ds((c * units + u) * wide + i, 1), :] for i in range(wide)], axis=1)
        for h in range(2):
            for b in range(chips):
                at = slice((h * chips + b) * sims, (h * chips + b + 1) * sims)
                total, last = keep[e, 0, at], None
                for t in range(1, chips):
                    s = h * chips + (b + t) % chips
                    term = far_r[q, t - 1, s * sims:(s + 1) * sims].astype(jnp.float32)
                    if b > 0 and t == chips - b:
                        last = term
                    else:
                        total = total + term
                if b > 0:
                    g_s[(b - 1) * 2 + h, u] = total.astype(jnp.bfloat16)
                    total = total + last
                elif h == 0:
                    out_ref[:, span(c, u)] = total
                else:
                    keep[e, 0, half:half + sims] = total
                    own_copy(u).start()
                w_v[at] = (weight * total).astype(jnp.bfloat16)
        proj_load(u).wait()
        tile = min(512, prows)
        for j in range(0, prows, tile):
            acc[:, j:j + tile] += lax.dot_general(w_v[...], proj_v[n, j:j + tile, :], NT, preferred_element_type=jnp.float32)

        @pl.when(u + 2 < units)
        def _():
            proj_load(u + 2).start()

    early = max(0, min((units + D2 - D3) // many, chunks - 1))

    def step(g, carry):
        @pl.when(g + 2 < units)
        def _():
            for cp in loads(g + 2):
                cp.start()

        @pl.when((g >= D2) & (g < units + D2))
        def _():
            sum_chip(g - D2)

        @pl.when(g < units)
        def _():
            multiply(g)

        @pl.when(g >= D3)
        def _():
            project(g - D3)

        @pl.when(g == units + D2 - 1)
        def _():
            for j in range(early):
                for cp in back_copies(j):
                    cp.start()

        return carry

    lax.fori_loop(0, units + D3, step, 0)

    hs, pb = sims // 2, prows // n_row
    pieces = [(t, h) for t in reversed(range(chips)) for h in range(2)]

    def swap_copy(i):
        t, h = pieces[i]
        return remote(acc.at[half + t * sims + h * hs:half + t * sims + (h + 1) * hs], swap.at[i], s1.at[i], r1.at[i], r, mate)

    def y_copy(i):
        return remote(fb.at[i, 1 - low], yb.at[i], s2.at[i], r2.at[i], beside, c)

    def z_copies(i):
        return [remote(gb.at[i, lax.rem(high + d, pairs)], zb.at[i, d - 1], s3.at[i, d - 1], r3.at[i, d - 1], lax.rem(high + d, pairs) * 2 + low, c)
                for d in range(1, pairs)]

    def x_copy(i):
        return remote(hb.at[i], xb.at[i], s4.at[i], r4.at[i], r, other(pieces[i][0], True))

    every = range(len(pieces))
    for i in every:
        swap_copy(i).start()
    for i in every:
        t, h = pieces[i]
        swap_copy(i).wait_recv()
        for k in range(n_row):
            fb[i, k % 2, k // 2] = acc[t * sims + h * hs:t * sims + (h + 1) * hs, k * pb:(k + 1) * pb] + swap[i, :, k * pb:(k + 1) * pb]
        y_copy(i).start()
    for i in every:
        y_copy(i).wait_recv()
        gb[i] = fb[i, low] + yb[i]
        for cp in z_copies(i):
            cp.start()
    for i in every:
        total = gb[i, high]
        for d, cp in enumerate(z_copies(i)):
            cp.wait_recv()
            total = total + zb[i, d]
        hb[i] = total
        if pieces[i][0] > 0:
            x_copy(i).start()
    for j in range(early, chunks):
        for cp in back_copies(j):
            cp.start()

    def finish(j):
        for cp in back_copies(j):
            cp.wait_recv()

        def one(u, carry):
            for cp in base_arrivals(u):
                cp.wait_recv()
            own_copy(u, False).wait_recv()
            for t in range(1, chips):
                for e in range(2):
                    at = span(other(chips - t, e == 0), u)
                    out_ref[:, at] = out_ref[:, at] + g_r[(t - 1) * 2 + e, u].astype(jnp.float32)
            return carry

        lax.fori_loop(j * many, (j + 1) * many, one, 0)

    for j in range(chunks - 1):
        finish(j)
    for h in range(2):
        total = hb[pieces.index((0, h))]
        for t in range(1, chips):
            i = pieces.index((t, h))
            x_copy(i).wait_recv()
            total = total + xb[i]
        pout_ref[h * hs:(h + 1) * hs, :] = total
    finish(chunks - 1)

    drain()
    for i in every:
        swap_copy(i).wait_send()
        y_copy(i).wait_send()
        for cp in z_copies(i):
            cp.wait_send()
        if pieces[i][0] > 0:
            x_copy(i).wait_send()
    for j in range(chunks):
        for cp in back_copies(j):
            cp.wait_send()
    for b in range(min(units, near_s.shape[0])):
        near_copy(units - 1 - b).wait_send()
    for b in range(min(units, far_s.shape[0])):
        for cp in far_copies(units - 1 - b):
            cp.wait_send()
    for b in range(min(units, keep.shape[0])):
        for cp in base_copies(units - 1 - b) + [own_copy(units - 1 - b)]:
            cp.wait_send()


def stream(index, maps, obs, prior, apod, proj, n_row, n_col):
    depth, (sims, rows), (prows, slab) = obs.shape[1], prior.shape, proj.shape
    panel, part = index.shape[0], index.shape[0] // n_row
    parts = max(1, LANES // sims)
    width = parts * math.gcd(UNIT, rows // parts)
    halves = 2
    size = math.gcd(slab, UNIT)
    units = slab // size
    chips, pairs = n_col // 2, n_row // 2
    all_sims, pb, hs, pieces = n_col * sims, prows // n_row, sims // 2, 2 * chips
    back = 2 * (chips - 1)
    chunks = 8 if units % 8 == 0 else units
    n_keep, n_far = D3 + 2, 2 * (D3 - D2) + 2
    vmem, anywhere = pl.BlockSpec(memory_space=pltpu.VMEM), pl.BlockSpec(memory_space=pltpu.HBM)
    dma, bf16, f32 = pltpu.SemaphoreType.DMA, jnp.bfloat16, jnp.float32
    return pl.pallas_call(
        functools.partial(stream_kernel, n_row, n_col, units),
        in_specs=[vmem] + [anywhere] * 5,
        out_specs=[vmem, vmem],
        out_shape=[jax.ShapeDtypeStruct((sims, rows), f32), jax.ShapeDtypeStruct((sims, pb), f32)],
        scratch_shapes=[
            pltpu.VMEM((rows // width, sims, width), bf16),
            pltpu.VMEM((rows // parts, parts * sims), f32),
            pltpu.VMEM((panel // LANES, LANES), jnp.int32),
            pltpu.SMEM((panel // LANES, LANES), jnp.int32),
            pltpu.VMEM((part, parts * sims), f32),
            pltpu.VMEM((n_row, halves, sims // halves, part), bf16),
            pltpu.VMEM((halves, n_row - 1, sims // halves, part), bf16),
            pltpu.VMEM((halves, sims // halves, part), bf16),
            pltpu.VMEM((n_row, halves, sims // halves, part), bf16),
            pltpu.VMEM((all_sims, depth), bf16),
            pltpu.VMEM((rows // LANES, LANES), f32),
            pltpu.VMEM((IN, n_col, size, depth), bf16),
            pltpu.VMEM((IN, n_col, sims, size), f32),
            pltpu.VMEM((IN, prows, size), bf16),
            pltpu.VMEM((2, chips, all_sims, size), f32),
            pltpu.VMEM((2 * D2, chips, all_sims, size), f32),
            pltpu.VMEM((n_keep, chips, all_sims, size), f32),
            pltpu.VMEM((SENDS, chips - 1, all_sims, size), bf16),
            pltpu.VMEM((n_far, chips - 1, all_sims, size), bf16),
            pltpu.VMEM((all_sims, size), bf16),
            pltpu.VMEM((all_sims, prows), f32),
            pltpu.VMEM((back, units, sims, size), bf16),
            pltpu.VMEM((back, units, sims, size), bf16),
            pltpu.VMEM((pieces, hs, prows), f32),
            pltpu.VMEM((pieces, 2, pairs, hs, pb), f32),
            pltpu.VMEM((pieces, pairs, hs, pb), f32),
            pltpu.VMEM((pieces, pairs, hs, pb), f32),
            pltpu.VMEM((pieces, pairs - 1, hs, pb), f32),
            pltpu.VMEM((pieces, hs, pb), f32),
            pltpu.VMEM((pieces, hs, pb), f32),
            pltpu.SemaphoreType.REGULAR, dma((rows // width,)), dma, dma((halves, n_row - 1)), dma((halves, n_row - 1)), dma((halves, n_row)), dma((halves, n_row)),
            dma, dma((IN, n_col)), dma((IN, n_col)), dma((IN,)), dma((2,)), dma((2 * D2,)),
            dma((SENDS, chips - 1)), dma((n_far, chips - 1)),
            dma((n_keep, chips - 1)), dma((units, chips - 1)), dma((n_keep,)), dma((units,)),
            dma((chunks, back)), dma((chunks, back)),
            dma((pieces,)), dma((pieces,)), dma((pieces,)), dma((pieces,)),
            dma((pieces, pairs - 1)), dma((pieces, pairs - 1)), dma((pieces,)), dma((pieces,)),
        ],
        compiler_params=pltpu.CompilerParams(has_side_effects=True, collective_id=0, vmem_limit_bytes=LIMIT),
        name="stream",
    )(index.reshape(panel // LANES, LANES), *[pltpu.with_memory_space_constraint(x, pltpu.HBM) for x in (maps, apod.reshape(rows // LANES, LANES), obs, prior, proj)])


def emit_kernel(out_ref, pout_ref, out, pout, sem):
    rows = math.gcd(out_ref.shape[0], 8)
    copies = [pltpu.make_async_copy(pout_ref, pout, sem.at[0])]
    for i in range(out_ref.shape[0] // rows):
        copies.append(pltpu.make_async_copy(out_ref.at[i * rows:(i + 1) * rows], out.at[i * rows:(i + 1) * rows], sem.at[i + 1]))
    for cp in copies:
        cp.start()
    for cp in copies:
        cp.wait()


def emit(out, pout):
    vmem, hbm = pl.BlockSpec(memory_space=pltpu.VMEM), pl.BlockSpec(memory_space=pltpu.HBM)
    return pl.pallas_call(
        emit_kernel,
        out_shape=[jax.ShapeDtypeStruct(x.shape, x.dtype) for x in (out, pout)],
        in_specs=[vmem] * 2,
        out_specs=[hbm] * 2,
        scratch_shapes=[pltpu.SemaphoreType.DMA((out.shape[0] // math.gcd(out.shape[0], 8) + 1,))],
        compiler_params=pltpu.CompilerParams(vmem_limit_bytes=8 * 1024 * 1024),
        name="emit",
    )(out, pout)


def on_device(n_row, n_col, obs_panel, skies, panel_index, prior_sum, apod, proj_panel):
    out, projection = emit(*stream(panel_index, skies.T, obs_panel, prior_sum.T, apod, proj_panel, n_row, n_col))
    return out.T, projection.T


def solution(mesh):
    in_specs = (P("row", "col"), P("row", "col"), P(), P("row", "col"), P("row"), P(None, ("row", "col")))
    out_specs = (P("row", "col"), P("row", "col"))
    body = functools.partial(on_device, mesh.shape["row"], mesh.shape["col"])
    return jax.shard_map(body, mesh=mesh, in_specs=in_specs, out_specs=out_specs, check_vma=False)
```

```python
import functools
import math

import jax
import jax.numpy as jnp
from jax import lax
from jax.experimental import pallas as pl
from jax.experimental.pallas import tpu as pltpu
from jax.sharding import PartitionSpec as P

MESH = pl.DeviceIdType.MESH
NT = (((1,), (1,)), ((), ()))
UNIT = 256
D2, D3 = 1, 4
SENDS, EARLY = 3, 2
LIMIT = 46 * 1024 * 1024
LANES = 128
AHEAD = 3


def remote(src, dst, send, recv, row, col):
    return pltpu.make_async_remote_copy(
        src_ref=src, dst_ref=dst, send_sem=send, recv_sem=recv, device_id=(row, col), device_id_type=MESH
    )


def greet(devices):
    for device in devices:
        pl.semaphore_signal(pltpu.get_barrier_semaphore(), inc=1, device_id=device, device_id_type=MESH)


def tabulate(r, idx_ref, held, table, where_v, where_s, loads, where_sem):
    groups, sims, width = held.shape
    rows, lanes = groups * width, table.shape[1]
    parts = lanes // sims
    span = width // parts
    at = idx_ref[...] - r * rows
    near = jnp.clip(at, 0, rows - 1)
    where_v[...] = lax.div(near, width) * span + lax.rem(near, span)
    codes = pltpu.make_async_copy(where_v, where_s, where_sem)
    codes.start()
    one = (lax.broadcasted_iota(jnp.int32, (span, span), 0) == lax.broadcasted_iota(jnp.int32, (span, span), 1)).astype(held.dtype)
    pair = 2 if groups % 2 == 0 else 1
    batch = max(1, groups // pair // 4) * pair
    for first in range(0, groups, batch):
        some = range(first, min(groups, first + batch))
        for g in some:
            loads[g].wait()
        for g in some[::pair]:
            block = jnp.concatenate([held[i, :, b * span:(b + 1) * span] for i in range(g, g + pair) for b in range(parts)], axis=0)
            turned = lax.dot_general(one, block, NT, preferred_element_type=jnp.float32)
            for i in range(pair):
                table[(g + i) * span:(g + i + 1) * span, :] = turned[:, i * lanes:(i + 1) * lanes]
    codes.wait()
    where_v[...] = jnp.where((at >= 0) & (at < rows), lax.rem(lax.div(near, span), parts), -1)


def spread(n_row, n_col, r, c, peers, ready, p_ref, table, where_v, where_s, rows_v, own, land, mine, gather, send1, recv1, send2, recv2):
    halves, sims, part = own.shape[1], own.shape[1] * own.shape[2], own.shape[3]
    hs, lanes, rep = sims // halves, table.shape[1], n_row // n_col
    tiles = part // LANES
    turn = (lax.broadcasted_iota(jnp.int32, (lanes, lanes), 0) == lax.broadcasted_iota(jnp.int32, (lanes, lanes), 1)).astype(own.dtype)

    def part_of(row):
        return lax.rem(row, 2) * (n_row // 2) + lax.div(row, 2)

    def first_copy(d, h):
        to = lax.rem(r + d, n_row)
        return remote(own.at[part_of(to), h], land.at[h, d - 1], send1.at[h, d - 1], recv1.at[h, d - 1], to, c)

    def collect(i, carry):
        d = lax.rem(i + 1, n_row)
        k = part_of(lax.rem(r + d, n_row))
        for t in range(tiles):
            for j in range(LANES):
                rows_v[t * LANES + j:t * LANES + j + 1, :] = table[pl.ds(where_s[k * tiles + t, j], 1), :]
        for t in range(tiles):
            flat = lax.dot_general(turn, rows_v[t * LANES:(t + 1) * LANES, :].astype(own.dtype), NT, preferred_element_type=jnp.float32)
            which = where_v[pl.ds(k * tiles + t, 1), :]
            total = jnp.zeros((sims, LANES), jnp.float32)
            for b in range(lanes // sims):
                total = jnp.where(which == b, flat[b * sims:(b + 1) * sims], total)
            for h in range(halves):
                own[k, h, :, t * LANES:(t + 1) * LANES] = total[h * hs:(h + 1) * hs].astype(own.dtype)

        return d

    def collect_and_send(i, carry):
        d = collect(i, carry)

        @pl.when(d > 0)
        def _():
            first_copy(d, 0).start()

        return carry

    ahead = min(AHEAD, n_row - 1)
    lax.fori_loop(0, ahead, lambda i, carry: (collect(i, carry), carry)[1], 0)
    pl.semaphore_wait(pltpu.get_barrier_semaphore(), n_row + n_col - 2)
    for device in peers:
        pl.semaphore_signal(ready, inc=1, device_id=device, device_id_type=MESH)
    for d in range(1, ahead + 1):
        first_copy(d, 0).start()
    lax.fori_loop(ahead, n_row, collect_and_send, 0)
    for h in range(1, halves):
        for d in range(1, n_row):
            first_copy(d, h).start()
    pl.semaphore_wait(ready, n_col - 1)
    sub, col_to = lax.rem(part_of(r), rep), lax.div(part_of(r), rep)
    slot = sub * n_col + c

    def second_copy(d, h):
        return remote(mine.at[h], gather.at[slot, h], send2.at[h, d], recv2.at[h, slot], lax.rem(r + d, n_row), col_to)

    for h in range(halves):
        total = own[part_of(r), h].astype(jnp.float32)
        for d in range(1, n_row):
            first_copy(d, h).wait_recv()
            total = total + land[h, d - 1].astype(jnp.float32)
        mine[h] = total.astype(mine.dtype)
        for d in range(1, n_row):
            second_copy(d, h).start()

        @pl.when(col_to != c)
        def _():
            second_copy(0, h).start()

        @pl.when(col_to == c)
        def _():
            gather[slot, h] = mine[h]

    chips = n_col // 2
    core, chip = lax.rem(c, 2), lax.div(c, 2)

    def arrive(h):
        for s in range(rep):
            for j in range(n_col):
                @pl.when(jnp.logical_not((c * rep + s == part_of(r)) & (c == j)))
                def _():
                    remote(mine.at[h], gather.at[s * n_col + j, h], send2.at[h, 0], recv2.at[h, s * n_col + j], r, c).wait_recv()
        for q in range(n_col):
            source = lax.rem(chip + q % chips, chips) * 2 + (core if q // chips == 0 else 1 - core)
            at = (h * n_col + q) * hs
            for s in range(rep):
                p_ref[at:at + hs, s * part:(s + 1) * part] = gather[s * n_col + source, h]

    def drain():
        for h in range(halves):
            for d in range(1, n_row):
                first_copy(d, h).wait_send()
                second_copy(d, h).wait_send()

            @pl.when(col_to != c)
            def _():
                second_copy(0, h).wait_send()

    return arrive, drain


def stream_kernel(n_row, n_col, units, idx_ref, maps, apod, obs, prior, proj, out_ref, pout_ref,
                  held, table, where_v, where_s, rows_v, own, land, mine, gather, p_ref,
                  apod_ref, obs_v, pri_v, proj_v, near_s, near_r, keep, base_s, own_s, far_s, far_r, w_v, acc, g_s, g_r,
                  swap, fb, yb, gb, zb, hb, xb,
                  ready, ms, ws, s5, r5, s6, r6, aps, os, ps, js, ns, nr, es, er, fs, fr, ds, dr, ts, tr, us, ur, gs, gr, s1, r1, s2, r2, s3, r3, s4, r4):
    r, c = lax.axis_index("row"), lax.axis_index("col")
    chips, pairs = n_col // 2, n_row // 2
    core, chip = lax.rem(c, 2), lax.div(c, 2)
    low, high = lax.rem(r, 2), lax.div(r, 2)
    mate, beside = chip * 2 + 1 - core, high * 2 + 1 - low
    sims, rows = out_ref.shape
    prows, slab = proj.shape
    size, hs = slab // units, sims // 2
    half, quad = n_col * hs, chips * hs
    start, keeps = min(EARLY, units // 4), keep.shape[0]
    hold, lent, stock = near_s.shape[0], far_s.shape[0], obs_v.shape[0]

    def other(t, same):
        return lax.rem(chip + t, chips) * 2 + (core if same else 1 - core)

    def span(q, u):
        return pl.ds(pl.multiple_of(q * slab + u * size, size), size)

    def loads(u):
        k, copies = lax.rem(u, stock), []
        for o in range(2):
            for t in range(chips):
                i, at = o * chips + t, span(other(t, o == 1), u)
                copies.append(pltpu.make_async_copy(obs.at[at, :], obs_v.at[k, i], os.at[k, i]))
                copies.append(pltpu.make_async_copy(prior.at[:, at], pri_v.at[k, i], ps.at[k, i]))
        return copies

    def proj_load(u):
        k = lax.rem(u, proj_v.shape[0])
        return pltpu.make_async_copy(proj.at[:, pl.ds(pl.multiple_of(u * size, size), size)], proj_v.at[k], js.at[k])

    def near_copy(u):
        k, q = lax.rem(u, near_s.shape[0]), lax.rem(u, near_r.shape[0])
        return remote(near_s.at[k], near_r.at[q], ns.at[k], nr.at[q], r, mate)

    def far_copies(u):
        k, q = lax.rem(u, far_s.shape[0]), lax.rem(u, far_r.shape[0])
        return [remote(far_s.at[k, t - 1], far_r.at[q, t - 1], fs.at[k, t - 1], fr.at[q, t - 1], r, other(t, True))
                for t in range(1, chips)]

    def near_half(u, h):
        k, q, at = lax.rem(u, hold), lax.rem(u, near_r.shape[0]), slice(h * half, (h + 1) * half)
        return remote(near_s.at[k, :, at], near_r.at[q, :, at], es.at[u, h], er.at[u, h], r, mate)

    def far_half(u, h):
        k, q, at = lax.rem(u, lent), lax.rem(u, far_r.shape[0]), slice(h * half, (h + 1) * half)
        return [remote(far_s.at[k, t - 1, at], far_r.at[q, t - 1, at], ds.at[u, h, t - 1], dr.at[u, h, t - 1], r, other(t, True))
                for t in range(1, chips)]

    def base_copies(u):
        k = lax.rem(u, keeps)
        return [remote(base_s.at[k, t - 1], out_ref.at[:, span(other(t, True), u)], ts.at[k, t - 1], tr.at[u, t - 1], r, mate)
                for t in range(1, chips)]

    def base_arrivals(u):
        return [remote(base_s.at[0, t - 1], out_ref.at[:, span(other(t, False), u)], ts.at[0, t - 1], tr.at[u, t - 1], r, mate)
                for t in range(1, chips)]

    def own_copy(u, same=True):
        k = lax.rem(u, keeps)
        return remote(own_s.at[k], out_ref.at[:, span(other(0, same), u)], us.at[k], ur.at[u], r, mate)

    chunks = 8 if units % 8 == 0 else units
    many = units // chunks

    def back_copies(j):
        at = pl.ds(j * many, many)
        return [remote(g_s.at[(t - 1) * 2 + e, at], g_r.at[(t - 1) * 2 + e, at], gs.at[j, (t - 1) * 2 + e], gr.at[j, (t - 1) * 2 + e], r, other(t, e == 0))
                for t in range(1, chips) for e in range(2)]

    width = held.shape[2]
    tables = [pltpu.make_async_copy(maps.at[:, g * width:(g + 1) * width], held.at[g], ms.at[g]) for g in range(held.shape[0])]
    weights = pltpu.make_async_copy(apod, apod_ref, aps)
    for cp in tables:
        cp.start()
    line, peers = [(lax.rem(r + d, n_row), c) for d in range(1, n_row)], [(r, lax.rem(c + d, n_col)) for d in range(1, n_col)]
    greet(line + peers)
    acc[...] = jnp.zeros_like(acc)
    tabulate(r, idx_ref, held, table, where_v, where_s, tables, ws)
    for cp in [weights] + [cp for u in range(min(start + 2, units)) for cp in loads(u)] + [proj_load(u) for u in range(min(2, units))]:
        cp.start()
    arrive, drain = spread(n_row, n_col, r, c, peers, ready, p_ref, table, where_v, where_s, rows_v, own, land, mine, gather, s5, r5, s6, r6)

    def sum_chip(u, halves=(0, 1)):
        k, q, e = lax.rem(u, lent), lax.rem(u, near_r.shape[0]), lax.rem(u, keeps)
        away = far_copies(u) if len(halves) == 2 else far_half(u, halves[0])
        base = base_copies(u) if halves[-1] == 1 else []
        for t in list(range(1, chips)) + [0]:
            for h in halves:
                b = h * half
                lo = keep[e, t, b:b + quad] + near_r[q, t, b + quad:b + half]
                hi = keep[e, t, b + quad:b + half] + near_r[q, t, b:b + quad]
                if t > 0:
                    far_s[k, t - 1, b:b + quad] = lo.astype(jnp.bfloat16)
                    far_s[k, t - 1, b + quad:b + half] = hi.astype(jnp.bfloat16)
                    out_ref[h * hs:(h + 1) * hs, span(other(t, True), u)] = lo[:hs]
                    base_s[e, t - 1, h * hs:(h + 1) * hs] = hi[:hs]
                else:
                    keep[e, 0, b:b + quad] = lo
                    keep[e, 0, b + quad:b + half] = hi
            if t > 0:
                away[t - 1].start()
                if base:
                    base[t - 1].start()

    def multiply(u, halves=(0, 1)):
        n, k, e = lax.rem(u, stock), lax.rem(u, hold), lax.rem(u, keeps)
        for o in range(2):
            for t in range(chips):
                value = lax.dot_general(p_ref[halves[0] * half:(halves[-1] + 1) * half, :], obs_v[n, o * chips + t], NT, preferred_element_type=jnp.float32)
                for i, h in enumerate(halves):
                    first = value[i * half:i * half + hs] + pri_v[n, o * chips + t, h * hs:(h + 1) * hs]
                    rest, b = value[i * half + hs:(i + 1) * half], h * half
                    if o == 0:
                        near_s[k, t, b:b + hs] = first
                        near_s[k, t, b + hs:b + half] = rest
                    else:
                        keep[e, t, b:b + hs] = first
                        keep[e, t, b + hs:b + half] = rest
            if o == 0:
                (near_copy(u) if len(halves) == 2 else near_half(u, halves[0])).start()

    def sum_next(u):
        near_copy(u).wait_recv()

        @pl.when(u >= lent + start)
        def _():
            for cp in far_copies(u - lent):
                cp.wait_send()

        if start:
            @pl.when((u >= lent) & (u < lent + start))
            def _():
                for h in range(2):
                    for cp in far_half(u - lent, h):
                        cp.wait_send()

        sum_chip(u)

    def multiply_next(u):
        for cp in loads(u):
            cp.wait()

        @pl.when(u >= hold + start)
        def _():
            near_copy(u - hold).wait_send()

        if start:
            @pl.when((u >= hold) & (u < hold + start))
            def _():
                for h in range(2):
                    near_half(u - hold, h).wait_send()

        @pl.when(u >= keeps)
        def _():
            for cp in base_copies(u - keeps) + [own_copy(u - keeps)]:
                cp.wait_send()

        multiply(u)

    def project(u):
        @pl.when(u >= start)
        def _():
            for cp in far_copies(u):
                cp.wait_recv()

        if start:
            @pl.when(u < start)
            def _():
                for h in range(2):
                    for cp in far_half(u, h):
                        cp.wait_recv()

        q, e, n = lax.rem(u, far_r.shape[0]), lax.rem(u, keeps), lax.rem(u, proj_v.shape[0])
        wide = size // LANES
        weight = jnp.concatenate([apod_ref[pl.ds((c * units + u) * wide + i, 1), :] for i in range(wide)], axis=1)
        for h in range(2):
            part = slice(h * hs, (h + 1) * hs)
            for f in range(2):
                for b in range(chips):
                    at = slice(h * half + (f * chips + b) * hs, h * half + (f * chips + b + 1) * hs)
                    total, last = keep[e, 0, at], None
                    for t in range(1, chips):
                        s = h * half + (f * chips + (b + t) % chips) * hs
                        term = far_r[q, t - 1, s:s + hs].astype(jnp.float32)
                        if b > 0 and t == chips - b:
                            last = term
                        else:
                            total = total + term
                    if b > 0:
                        g_s[(b - 1) * 2 + f, u, part] = total.astype(jnp.bfloat16)
                        total = total + last
                    elif f == 0:
                        out_ref[part, span(c, u)] = total
                    else:
                        own_s[e, part] = total
                    w_v[at] = (weight * total).astype(jnp.bfloat16)
        own_copy(u).start()
        proj_load(u).wait()
        tile = min(512, prows)
        for j in range(0, prows, tile):
            acc[:, j:j + tile] += lax.dot_general(w_v[...], proj_v[n, j:j + tile, :], NT, preferred_element_type=jnp.float32)

        @pl.when(u + 2 < units)
        def _():
            proj_load(u + 2).start()

    early = max(0, min((units + D2 - D3) // many, chunks - 1))

    def step(g, carry):
        @pl.when(g + 2 < units)
        def _():
            for cp in loads(g + 2):
                cp.start()

        @pl.when((g >= start + D2) & (g < units + D2))
        def _():
            sum_next(g - D2)

        @pl.when(g < units)
        def _():
            multiply_next(g)

        @pl.when(g >= D3)
        def _():
            project(g - D3)

        @pl.when(g == units + D2 - 1)
        def _():
            for j in range(early):
                for cp in back_copies(j):
                    cp.start()

        return carry

    for h in range(2):
        arrive(h)
        for i in range(start + 1):
            if i < start:
                if h == 0:
                    for cp in loads(i):
                        cp.wait()
                multiply(i, (h,))
            if 0 < i:
                near_half(i - 1, h).wait_recv()
                sum_chip(i - 1, (h,))
    weights.wait()
    lax.fori_loop(start, units + D3, step, 0)

    pb = prows // n_row
    pieces = [(t, h) for t in reversed(range(chips)) for h in range(2)]

    def swap_copy(i):
        t, h = pieces[i]
        return remote(acc.at[h * half + quad + t * hs:h * half + quad + (t + 1) * hs], swap.at[i], s1.at[i], r1.at[i], r, mate)

    def y_copy(i):
        return remote(fb.at[i, 1 - low], yb.at[i], s2.at[i], r2.at[i], beside, c)

    def z_copies(i):
        return [remote(gb.at[i, lax.rem(high + d, pairs)], zb.at[i, d - 1], s3.at[i, d - 1], r3.at[i, d - 1], lax.rem(high + d, pairs) * 2 + low, c)
                for d in range(1, pairs)]

    def x_copy(i):
        return remote(hb.at[i], xb.at[i], s4.at[i], r4.at[i], r, other(pieces[i][0], True))

    every = range(len(pieces))
    for i in every:
        swap_copy(i).start()
    for i in every:
        t, h = pieces[i]
        swap_copy(i).wait_recv()
        for k in range(n_row):
            fb[i, k % 2, k // 2] = acc[h * half + t * hs:h * half + (t + 1) * hs, k * pb:(k + 1) * pb] + swap[i, :, k * pb:(k + 1) * pb]
        y_copy(i).start()
    for i in every:
        y_copy(i).wait_recv()
        gb[i] = fb[i, low] + yb[i]
        for cp in z_copies(i):
            cp.start()
    for i in every:
        total = gb[i, high]
        for d, cp in enumerate(z_copies(i)):
            cp.wait_recv()
            total = total + zb[i, d]
        hb[i] = total
        if pieces[i][0] > 0:
            x_copy(i).start()
    for j in range(early, chunks):
        for cp in back_copies(j):
            cp.start()

    def finish(j):
        for cp in back_copies(j):
            cp.wait_recv()

        def one(u, carry):
            for cp in base_arrivals(u):
                cp.wait_recv()
            own_copy(u, False).wait_recv()
            for t in range(1, chips):
                for e in range(2):
                    at = span(other(chips - t, e == 0), u)
                    out_ref[:, at] = out_ref[:, at] + g_r[(t - 1) * 2 + e, u].astype(jnp.float32)
            return carry

        lax.fori_loop(j * many, (j + 1) * many, one, 0)

    for j in range(chunks - 1):
        finish(j)
    for h in range(2):
        total = hb[pieces.index((0, h))]
        for t in range(1, chips):
            i = pieces.index((t, h))
            x_copy(i).wait_recv()
            total = total + xb[i]
        pout_ref[h * hs:(h + 1) * hs, :] = total
    finish(chunks - 1)

    drain()
    for i in every:
        swap_copy(i).wait_send()
        y_copy(i).wait_send()
        for cp in z_copies(i):
            cp.wait_send()
        if pieces[i][0] > 0:
            x_copy(i).wait_send()
    for j in range(chunks):
        for cp in back_copies(j):
            cp.wait_send()
    for b in range(min(units, near_s.shape[0])):
        near_copy(units - 1 - b).wait_send()
    for b in range(min(units, far_s.shape[0])):
        for cp in far_copies(units - 1 - b):
            cp.wait_send()
    for b in range(min(units, keep.shape[0])):
        for cp in base_copies(units - 1 - b) + [own_copy(units - 1 - b)]:
            cp.wait_send()


def stream(index, maps, obs, prior, apod, proj, n_row, n_col):
    depth, (sims, rows), (prows, slab) = obs.shape[1], prior.shape, proj.shape
    panel, part = index.shape[0], index.shape[0] // n_row
    parts = max(1, LANES // sims)
    width = parts * math.gcd(UNIT, rows // parts)
    halves = 2
    size = math.gcd(slab, UNIT)
    units = slab // size
    chips, pairs = n_col // 2, n_row // 2
    all_sims, pb, hs, pieces = n_col * sims, prows // n_row, sims // 2, 2 * chips
    back = 2 * (chips - 1)
    chunks = 8 if units % 8 == 0 else units
    n_keep, n_far = D3 + 2, 2 * (D3 - D2) + 2
    start = min(EARLY, units // 4)
    hold, lent, stock = max(2, start + 1), max(SENDS, start), max(3, start + 2)
    vmem, anywhere = pl.BlockSpec(memory_space=pltpu.VMEM), pl.BlockSpec(memory_space=pltpu.HBM)
    dma, bf16, f32 = pltpu.SemaphoreType.DMA, jnp.bfloat16, jnp.float32
    return pl.pallas_call(
        functools.partial(stream_kernel, n_row, n_col, units),
        in_specs=[vmem] + [anywhere] * 5,
        out_specs=[vmem, vmem],
        out_shape=[jax.ShapeDtypeStruct((sims, rows), f32), jax.ShapeDtypeStruct((sims, pb), f32)],
        scratch_shapes=[
            pltpu.VMEM((rows // width, sims, width), bf16),
            pltpu.VMEM((rows // parts, parts * sims), f32),
            pltpu.VMEM((panel // LANES, LANES), jnp.int32),
            pltpu.SMEM((panel // LANES, LANES), jnp.int32),
            pltpu.VMEM((part, parts * sims), f32),
            pltpu.VMEM((n_row, halves, sims // halves, part), bf16),
            pltpu.VMEM((halves, n_row - 1, sims // halves, part), bf16),
            pltpu.VMEM((halves, sims // halves, part), bf16),
            pltpu.VMEM((n_row, halves, sims // halves, part), bf16),
            pltpu.VMEM((all_sims, depth), bf16),
            pltpu.VMEM((rows // LANES, LANES), f32),
            pltpu.VMEM((stock, n_col, size, depth), bf16),
            pltpu.VMEM((stock, n_col, sims, size), f32),
            pltpu.VMEM((3, prows, size), bf16),
            pltpu.VMEM((hold, chips, all_sims, size), f32),
            pltpu.VMEM((hold, chips, all_sims, size), f32),
            pltpu.VMEM((n_keep, chips, all_sims, size), f32),
            pltpu.VMEM((n_keep, chips - 1, sims, size), f32),
            pltpu.VMEM((n_keep, sims, size), f32),
            pltpu.VMEM((lent, chips - 1, all_sims, size), bf16),
            pltpu.VMEM((n_far, chips - 1, all_sims, size), bf16),
            pltpu.VMEM((all_sims, size), bf16),
            pltpu.VMEM((all_sims, prows), f32),
            pltpu.VMEM((back, units, sims, size), bf16),
            pltpu.VMEM((back, units, sims, size), bf16),
            pltpu.VMEM((pieces, hs, prows), f32),
            pltpu.VMEM((pieces, 2, pairs, hs, pb), f32),
            pltpu.VMEM((pieces, pairs, hs, pb), f32),
            pltpu.VMEM((pieces, pairs, hs, pb), f32),
            pltpu.VMEM((pieces, pairs - 1, hs, pb), f32),
            pltpu.VMEM((pieces, hs, pb), f32),
            pltpu.VMEM((pieces, hs, pb), f32),
            pltpu.SemaphoreType.REGULAR, dma((rows // width,)), dma, dma((halves, n_row - 1)), dma((halves, n_row - 1)), dma((halves, n_row)), dma((halves, n_row)),
            dma, dma((stock, n_col)), dma((stock, n_col)), dma((3,)), dma((hold,)), dma((hold,)),
            dma((max(1, start), 2)), dma((max(1, start), 2)),
            dma((lent, chips - 1)), dma((n_far, chips - 1)),
            dma((max(1, start), 2, chips - 1)), dma((max(1, start), 2, chips - 1)),
            dma((n_keep, chips - 1)), dma((units, chips - 1)), dma((n_keep,)), dma((units,)),
            dma((chunks, back)), dma((chunks, back)),
            dma((pieces,)), dma((pieces,)), dma((pieces,)), dma((pieces,)),
            dma((pieces, pairs - 1)), dma((pieces, pairs - 1)), dma((pieces,)), dma((pieces,)),
        ],
        compiler_params=pltpu.CompilerParams(has_side_effects=True, collective_id=0, vmem_limit_bytes=LIMIT),
        name="stream",
    )(index.reshape(panel // LANES, LANES), *[pltpu.with_memory_space_constraint(x, pltpu.HBM) for x in (maps, apod.reshape(rows // LANES, LANES), obs, prior, proj)])


def emit_kernel(out_ref, pout_ref, out, pout, sem):
    rows = math.gcd(out_ref.shape[0], 8)
    copies = [pltpu.make_async_copy(pout_ref, pout, sem.at[0])]
    for i in range(out_ref.shape[0] // rows):
        copies.append(pltpu.make_async_copy(out_ref.at[i * rows:(i + 1) * rows], out.at[i * rows:(i + 1) * rows], sem.at[i + 1]))
    for cp in copies:
        cp.start()
    for cp in copies:
        cp.wait()


def emit(out, pout):
    vmem, hbm = pl.BlockSpec(memory_space=pltpu.VMEM), pl.BlockSpec(memory_space=pltpu.HBM)
    return pl.pallas_call(
        emit_kernel,
        out_shape=[jax.ShapeDtypeStruct(x.shape, x.dtype) for x in (out, pout)],
        in_specs=[vmem] * 2,
        out_specs=[hbm] * 2,
        scratch_shapes=[pltpu.SemaphoreType.DMA((out.shape[0] // math.gcd(out.shape[0], 8) + 1,))],
        compiler_params=pltpu.CompilerParams(vmem_limit_bytes=8 * 1024 * 1024),
        name="emit",
    )(out, pout)


def on_device(n_row, n_col, obs_panel, skies, panel_index, prior_sum, apod, proj_panel):
    out, projection = emit(*stream(panel_index, skies.T, obs_panel, prior_sum.T, apod, proj_panel, n_row, n_col))
    return out.T, projection.T


def solution(mesh):
    in_specs = (P("row", "col"), P("row", "col"), P(), P("row", "col"), P("row"), P(None, ("row", "col")))
    out_specs = (P("row", "col"), P("row", "col"))
    body = functools.partial(on_device, mesh.shape["row"], mesh.shape["col"])
    return jax.shard_map(body, mesh=mesh, in_specs=in_specs, out_specs=out_specs, check_vma=False)
```

```python
import functools
import math

import jax
import jax.numpy as jnp
from jax import lax
from jax.experimental import pallas as pl
from jax.experimental.pallas import tpu as pltpu
from jax.sharding import PartitionSpec as P

MESH = pl.DeviceIdType.MESH
NT = (((1,), (1,)), ((), ()))
UNIT = 256
D2, D3 = 1, 4
SENDS, EARLY = 3, 2
LIMIT = 46 * 1024 * 1024
LANES = 128
EMIT_ROWS, EMIT_COLS = 2, 1
AHEAD = 3


def remote(src, dst, send, recv, row, col):
    return pltpu.make_async_remote_copy(
        src_ref=src, dst_ref=dst, send_sem=send, recv_sem=recv, device_id=(row, col), device_id_type=MESH
    )


def greet(devices):
    for device in devices:
        pl.semaphore_signal(pltpu.get_barrier_semaphore(), inc=1, device_id=device, device_id_type=MESH)


def tabulate(r, idx_ref, held, table, where_v, where_s, loads, where_sem):
    groups, sims, width = held.shape
    rows, lanes = groups * width, table.shape[1]
    parts = lanes // sims
    span = width // parts
    at = idx_ref[...] - r * rows
    near = jnp.clip(at, 0, rows - 1)
    where_v[...] = lax.div(near, width) * span + lax.rem(near, span)
    codes = pltpu.make_async_copy(where_v, where_s, where_sem)
    codes.start()
    one = (lax.broadcasted_iota(jnp.int32, (span, span), 0) == lax.broadcasted_iota(jnp.int32, (span, span), 1)).astype(held.dtype)
    pair = 2 if groups % 2 == 0 else 1
    batch = max(1, groups // pair // 4) * pair
    for first in range(0, groups, batch):
        some = range(first, min(groups, first + batch))
        for g in some:
            loads[g].wait()
        for g in some[::pair]:
            block = jnp.concatenate([held[i, :, b * span:(b + 1) * span] for i in range(g, g + pair) for b in range(parts)], axis=0)
            turned = lax.dot_general(one, block, NT, preferred_element_type=jnp.float32)
            for i in range(pair):
                table[(g + i) * span:(g + i + 1) * span, :] = turned[:, i * lanes:(i + 1) * lanes]
    codes.wait()
    where_v[...] = jnp.where((at >= 0) & (at < rows), lax.rem(lax.div(near, span), parts), -1)


def spread(n_row, n_col, r, c, peers, ready, p_ref, table, where_v, where_s, rows_v, own, land, mine, gather, send1, recv1, send2, recv2):
    halves, sims, part = own.shape[1], own.shape[1] * own.shape[2], own.shape[3]
    hs, lanes, rep = sims // halves, table.shape[1], n_row // n_col
    tiles = part // LANES
    turn = (lax.broadcasted_iota(jnp.int32, (lanes, lanes), 0) == lax.broadcasted_iota(jnp.int32, (lanes, lanes), 1)).astype(own.dtype)

    def part_of(row):
        return lax.rem(row, 2) * (n_row // 2) + lax.div(row, 2)

    def first_copy(d, h):
        to = lax.rem(r + d, n_row)
        return remote(own.at[part_of(to), h], land.at[h, d - 1], send1.at[h, d - 1], recv1.at[h, d - 1], to, c)

    def collect(i, carry):
        d = lax.rem(i + 1, n_row)
        k = part_of(lax.rem(r + d, n_row))
        for t in range(tiles):
            for j in range(LANES):
                rows_v[t * LANES + j:t * LANES + j + 1, :] = table[pl.ds(where_s[k * tiles + t, j], 1), :]
            flat = lax.dot_general(turn, rows_v[t * LANES:(t + 1) * LANES, :].astype(own.dtype), NT, preferred_element_type=jnp.float32)
            which = where_v[pl.ds(k * tiles + t, 1), :]
            total = jnp.zeros((sims, LANES), jnp.float32)
            for b in range(lanes // sims):
                total = jnp.where(which == b, flat[b * sims:(b + 1) * sims], total)
            for h in range(halves):
                own[k, h, :, t * LANES:(t + 1) * LANES] = total[h * hs:(h + 1) * hs].astype(own.dtype)

        return d

    def collect_and_send(i, carry):
        d = collect(i, carry)

        @pl.when(d > 0)
        def _():
            first_copy(d, 0).start()

        return carry

    ahead = min(AHEAD, n_row - 1)
    lax.fori_loop(0, ahead, lambda i, carry: (collect(i, carry), carry)[1], 0)
    pl.semaphore_wait(pltpu.get_barrier_semaphore(), n_row + n_col - 2)
    for device in peers:
        pl.semaphore_signal(ready, inc=1, device_id=device, device_id_type=MESH)
    for d in range(1, ahead + 1):
        first_copy(d, 0).start()
    lax.fori_loop(ahead, n_row, collect_and_send, 0)
    for h in range(1, halves):
        for d in range(1, n_row):
            first_copy(d, h).start()
    pl.semaphore_wait(ready, n_col - 1)
    sub, col_to = lax.rem(part_of(r), rep), lax.div(part_of(r), rep)
    slot = sub * n_col + c

    def second_copy(d, h):
        return remote(mine.at[h], gather.at[slot, h], send2.at[h, d], recv2.at[h, slot], lax.rem(r + d, n_row), col_to)

    for h in range(halves):
        total = own[part_of(r), h].astype(jnp.float32)
        for d in range(1, n_row):
            first_copy(d, h).wait_recv()
            total = total + land[h, d - 1].astype(jnp.float32)
        mine[h] = total.astype(mine.dtype)
        for d in range(1, n_row):
            second_copy(d, h).start()

        @pl.when(col_to != c)
        def _():
            second_copy(0, h).start()

        @pl.when(col_to == c)
        def _():
            gather[slot, h] = mine[h]

    chips = n_col // 2
    core, chip = lax.rem(c, 2), lax.div(c, 2)

    def arrive(h):
        for s in range(rep):
            for j in range(n_col):
                @pl.when(jnp.logical_not((c * rep + s == part_of(r)) & (c == j)))
                def _():
                    remote(mine.at[h], gather.at[s * n_col + j, h], send2.at[h, 0], recv2.at[h, s * n_col + j], r, c).wait_recv()
        for q in range(n_col):
            source = lax.rem(chip + q % chips, chips) * 2 + (core if q // chips == 0 else 1 - core)
            at = (h * n_col + q) * hs
            for s in range(rep):
                p_ref[at:at + hs, s * part:(s + 1) * part] = gather[s * n_col + source, h]

    def drain():
        for h in range(halves):
            for d in range(1, n_row):
                first_copy(d, h).wait_send()
                second_copy(d, h).wait_send()

            @pl.when(col_to != c)
            def _():
                second_copy(0, h).wait_send()

    return arrive, drain


def stream_kernel(n_row, n_col, units, idx_ref, maps, apod, obs, prior, proj, out_ref, pout_ref,
                  held, table, where_v, where_s, rows_v, own, land, mine, gather, p_ref,
                  apod_ref, obs_v, pri_v, proj_v, near_s, near_r, keep, base_s, own_s, far_s, far_r, w_v, acc, g_s, g_r,
                  swap, fb, yb, gb, zb, hb, xb,
                  ready, ms, ws, s5, r5, s6, r6, aps, os, ps, js, ns, nr, es, er, fs, fr, ds, dr, ts, tr, us, ur, gs, gr, s1, r1, s2, r2, s3, r3, s4, r4):
    r, c = lax.axis_index("row"), lax.axis_index("col")
    chips, pairs = n_col // 2, n_row // 2
    core, chip = lax.rem(c, 2), lax.div(c, 2)
    low, high = lax.rem(r, 2), lax.div(r, 2)
    mate, beside = chip * 2 + 1 - core, high * 2 + 1 - low
    sims, rows = out_ref.shape
    prows, slab = proj.shape
    size, hs = slab // units, sims // 2
    half, quad = n_col * hs, chips * hs
    start, keeps = min(EARLY, units // 4), keep.shape[0]
    hold, lent, stock = near_s.shape[0], far_s.shape[0], obs_v.shape[0]

    def other(t, same):
        return lax.rem(chip + t, chips) * 2 + (core if same else 1 - core)

    def span(q, u):
        return pl.ds(pl.multiple_of(q * slab + u * size, size), size)

    def loads(u):
        k, copies = lax.rem(u, stock), []
        for o in range(2):
            for t in range(chips):
                i, at = o * chips + t, span(other(t, o == 1), u)
                copies.append(pltpu.make_async_copy(obs.at[at, :], obs_v.at[k, i], os.at[k, i]))
                copies.append(pltpu.make_async_copy(prior.at[:, at], pri_v.at[k, i], ps.at[k, i]))
        return copies

    def proj_load(u):
        k = lax.rem(u, proj_v.shape[0])
        return pltpu.make_async_copy(proj.at[:, pl.ds(pl.multiple_of(u * size, size), size)], proj_v.at[k], js.at[k])

    def near_copy(u):
        k, q = lax.rem(u, near_s.shape[0]), lax.rem(u, near_r.shape[0])
        return remote(near_s.at[k], near_r.at[q], ns.at[k], nr.at[q], r, mate)

    def far_copies(u):
        k, q = lax.rem(u, far_s.shape[0]), lax.rem(u, far_r.shape[0])
        return [remote(far_s.at[k, t - 1], far_r.at[q, t - 1], fs.at[k, t - 1], fr.at[q, t - 1], r, other(t, True))
                for t in range(1, chips)]

    def near_half(u, h):
        k, q, at = lax.rem(u, hold), lax.rem(u, near_r.shape[0]), slice(h * half, (h + 1) * half)
        return remote(near_s.at[k, :, at], near_r.at[q, :, at], es.at[u, h], er.at[u, h], r, mate)

    def far_half(u, h):
        k, q, at = lax.rem(u, lent), lax.rem(u, far_r.shape[0]), slice(h * half, (h + 1) * half)
        return [remote(far_s.at[k, t - 1, at], far_r.at[q, t - 1, at], ds.at[u, h, t - 1], dr.at[u, h, t - 1], r, other(t, True))
                for t in range(1, chips)]

    def base_copies(u):
        k = lax.rem(u, keeps)
        return [remote(base_s.at[k, t - 1], out_ref.at[:, span(other(t, True), u)], ts.at[k, t - 1], tr.at[u, t - 1], r, mate)
                for t in range(1, chips)]

    def base_arrivals(u):
        return [remote(base_s.at[0, t - 1], out_ref.at[:, span(other(t, False), u)], ts.at[0, t - 1], tr.at[u, t - 1], r, mate)
                for t in range(1, chips)]

    def own_copy(u, same=True):
        k = lax.rem(u, keeps)
        return remote(own_s.at[k], out_ref.at[:, span(other(0, same), u)], us.at[k], ur.at[u], r, mate)

    chunks = 8 if units % 8 == 0 else units
    many = units // chunks

    def back_copies(j):
        at = pl.ds(j * many, many)
        return [remote(g_s.at[(t - 1) * 2 + e, at], g_r.at[(t - 1) * 2 + e, at], gs.at[j, (t - 1) * 2 + e], gr.at[j, (t - 1) * 2 + e], r, other(t, e == 0))
                for t in range(1, chips) for e in range(2)]

    width = held.shape[2]
    tables = [pltpu.make_async_copy(maps.at[:, g * width:(g + 1) * width], held.at[g], ms.at[g]) for g in range(held.shape[0])]
    weights = pltpu.make_async_copy(apod, apod_ref, aps)
    for cp in tables:
        cp.start()
    line, peers = [(lax.rem(r + d, n_row), c) for d in range(1, n_row)], [(r, lax.rem(c + d, n_col)) for d in range(1, n_col)]
    greet(line + peers)
    acc[...] = jnp.zeros_like(acc)
    tabulate(r, idx_ref, held, table, where_v, where_s, tables, ws)
    for cp in [weights] + [cp for u in range(min(start + 2, units)) for cp in loads(u)] + [proj_load(u) for u in range(min(2, units))]:
        cp.start()
    arrive, drain = spread(n_row, n_col, r, c, peers, ready, p_ref, table, where_v, where_s, rows_v, own, land, mine, gather, s5, r5, s6, r6)

    def sum_chip(u, halves=(0, 1)):
        k, q, e = lax.rem(u, lent), lax.rem(u, near_r.shape[0]), lax.rem(u, keeps)
        away = far_copies(u) if len(halves) == 2 else far_half(u, halves[0])
        base = base_copies(u) if halves[-1] == 1 else []
        for t in list(range(1, chips)) + [0]:
            for h in halves:
                b = h * half
                lo = keep[e, t, b:b + quad] + near_r[q, t, b + quad:b + half]
                hi = keep[e, t, b + quad:b + half] + near_r[q, t, b:b + quad]
                if t > 0:
                    far_s[k, t - 1, b:b + quad] = lo.astype(jnp.bfloat16)
                    far_s[k, t - 1, b + quad:b + half] = hi.astype(jnp.bfloat16)
                    out_ref[h * hs:(h + 1) * hs, span(other(t, True), u)] = lo[:hs]
                    base_s[e, t - 1, h * hs:(h + 1) * hs] = hi[:hs]
                else:
                    keep[e, 0, b:b + quad] = lo
                    keep[e, 0, b + quad:b + half] = hi
            if t > 0:
                away[t - 1].start()
                if base:
                    base[t - 1].start()

    def multiply(u, halves=(0, 1)):
        n, k, e = lax.rem(u, stock), lax.rem(u, hold), lax.rem(u, keeps)
        for o in range(2):
            for t in range(chips):
                value = lax.dot_general(p_ref[halves[0] * half:(halves[-1] + 1) * half, :], obs_v[n, o * chips + t], NT, preferred_element_type=jnp.float32)
                for i, h in enumerate(halves):
                    first = value[i * half:i * half + hs] + pri_v[n, o * chips + t, h * hs:(h + 1) * hs]
                    rest, b = value[i * half + hs:(i + 1) * half], h * half
                    if o == 0:
                        near_s[k, t, b:b + hs] = first
                        near_s[k, t, b + hs:b + half] = rest
                    else:
                        keep[e, t, b:b + hs] = first
                        keep[e, t, b + hs:b + half] = rest
            if o == 0:
                (near_copy(u) if len(halves) == 2 else near_half(u, halves[0])).start()

    def sum_next(u):
        near_copy(u).wait_recv()

        @pl.when(u >= lent + start)
        def _():
            for cp in far_copies(u - lent):
                cp.wait_send()

        if start:
            @pl.when((u >= lent) & (u < lent + start))
            def _():
                for h in range(2):
                    for cp in far_half(u - lent, h):
                        cp.wait_send()

        sum_chip(u)

    def multiply_next(u):
        for cp in loads(u):
            cp.wait()

        @pl.when(u >= hold + start)
        def _():
            near_copy(u - hold).wait_send()

        if start:
            @pl.when((u >= hold) & (u < hold + start))
            def _():
                for h in range(2):
                    near_half(u - hold, h).wait_send()

        @pl.when(u >= keeps)
        def _():
            for cp in base_copies(u - keeps) + [own_copy(u - keeps)]:
                cp.wait_send()

        multiply(u)

    def project(u):
        @pl.when(u >= start)
        def _():
            for cp in far_copies(u):
                cp.wait_recv()

        if start:
            @pl.when(u < start)
            def _():
                for h in range(2):
                    for cp in far_half(u, h):
                        cp.wait_recv()

        q, e, n = lax.rem(u, far_r.shape[0]), lax.rem(u, keeps), lax.rem(u, proj_v.shape[0])
        wide = size // LANES
        weight = jnp.concatenate([apod_ref[pl.ds((c * units + u) * wide + i, 1), :] for i in range(wide)], axis=1)
        for h in range(2):
            part = slice(h * hs, (h + 1) * hs)
            for f in range(2):
                for b in range(chips):
                    at = slice(h * half + (f * chips + b) * hs, h * half + (f * chips + b + 1) * hs)
                    total, last = keep[e, 0, at], None
                    for t in range(1, chips):
                        s = h * half + (f * chips + (b + t) % chips) * hs
                        term = far_r[q, t - 1, s:s + hs].astype(jnp.float32)
                        if b > 0 and t == chips - b:
                            last = term
                        else:
                            total = total + term
                    if b > 0:
                        g_s[(b - 1) * 2 + f, u, part] = total.astype(jnp.bfloat16)
                        total = total + last
                    elif f == 0:
                        out_ref[part, span(c, u)] = total
                    else:
                        own_s[e, part] = total
                    w_v[at] = (weight * total).astype(jnp.bfloat16)
        own_copy(u).start()
        proj_load(u).wait()
        tile = min(512, prows)
        for j in range(0, prows, tile):
            acc[:, j:j + tile] += lax.dot_general(w_v[...], proj_v[n, j:j + tile, :], NT, preferred_element_type=jnp.float32)

        @pl.when(u + 2 < units)
        def _():
            proj_load(u + 2).start()

    early = max(0, min((units + D2 - D3) // many, chunks - 1))

    def step(g, carry):
        @pl.when(g + 2 < units)
        def _():
            for cp in loads(g + 2):
                cp.start()

        @pl.when((g >= start + D2) & (g < units + D2))
        def _():
            sum_next(g - D2)

        @pl.when(g < units)
        def _():
            multiply_next(g)

        @pl.when(g >= D3)
        def _():
            project(g - D3)

        @pl.when(g == units + D2 - 1)
        def _():
            for j in range(early):
                for cp in back_copies(j):
                    cp.start()

        return carry

    for h in range(2):
        arrive(h)
        for i in range(start + 1):
            if i < start:
                if h == 0:
                    for cp in loads(i):
                        cp.wait()
                multiply(i, (h,))
            if 0 < i:
                near_half(i - 1, h).wait_recv()
                sum_chip(i - 1, (h,))
    weights.wait()
    lax.fori_loop(start, units + D3, step, 0)

    pb = prows // n_row
    pieces = [(t, h) for t in reversed(range(chips)) for h in range(2)]

    def swap_copy(i):
        t, h = pieces[i]
        return remote(acc.at[h * half + quad + t * hs:h * half + quad + (t + 1) * hs], swap.at[i], s1.at[i], r1.at[i], r, mate)

    def y_copy(i):
        return remote(fb.at[i, 1 - low], yb.at[i], s2.at[i], r2.at[i], beside, c)

    def z_copies(i):
        return [remote(gb.at[i, lax.rem(high + d, pairs)], zb.at[i, d - 1], s3.at[i, d - 1], r3.at[i, d - 1], lax.rem(high + d, pairs) * 2 + low, c)
                for d in range(1, pairs)]

    def x_copy(i):
        return remote(hb.at[i], xb.at[i], s4.at[i], r4.at[i], r, other(pieces[i][0], True))

    every = range(len(pieces))
    for i in every:
        swap_copy(i).start()
    for i in every:
        t, h = pieces[i]
        swap_copy(i).wait_recv()
        for k in range(n_row):
            fb[i, k % 2, k // 2] = acc[h * half + t * hs:h * half + (t + 1) * hs, k * pb:(k + 1) * pb] + swap[i, :, k * pb:(k + 1) * pb]
        y_copy(i).start()
    for i in every:
        y_copy(i).wait_recv()
        gb[i] = fb[i, low] + yb[i]
        for cp in z_copies(i):
            cp.start()
    for i in every:
        total = gb[i, high]
        for d, cp in enumerate(z_copies(i)):
            cp.wait_recv()
            total = total + zb[i, d]
        hb[i] = total
        if pieces[i][0] > 0:
            x_copy(i).start()
    for j in range(early, chunks):
        for cp in back_copies(j):
            cp.start()

    def finish(j):
        for cp in back_copies(j):
            cp.wait_recv()

        def one(u, carry):
            for cp in base_arrivals(u):
                cp.wait_recv()
            own_copy(u, False).wait_recv()
            for t in range(1, chips):
                for e in range(2):
                    at = span(other(chips - t, e == 0), u)
                    out_ref[:, at] = out_ref[:, at] + g_r[(t - 1) * 2 + e, u].astype(jnp.float32)
            return carry

        lax.fori_loop(j * many, (j + 1) * many, one, 0)

    for j in range(chunks - 1):
        finish(j)
    for h in range(2):
        total = hb[pieces.index((0, h))]
        for t in range(1, chips):
            i = pieces.index((t, h))
            x_copy(i).wait_recv()
            total = total + xb[i]
        pout_ref[h * hs:(h + 1) * hs, :] = total
    finish(chunks - 1)

    drain()
    for i in every:
        swap_copy(i).wait_send()
        y_copy(i).wait_send()
        for cp in z_copies(i):
            cp.wait_send()
        if pieces[i][0] > 0:
            x_copy(i).wait_send()
    for j in range(chunks):
        for cp in back_copies(j):
            cp.wait_send()
    for b in range(min(units, near_s.shape[0])):
        near_copy(units - 1 - b).wait_send()
    for b in range(min(units, far_s.shape[0])):
        for cp in far_copies(units - 1 - b):
            cp.wait_send()
    for b in range(min(units, keep.shape[0])):
        for cp in base_copies(units - 1 - b) + [own_copy(units - 1 - b)]:
            cp.wait_send()


def stream(index, maps, obs, prior, apod, proj, n_row, n_col):
    depth, (sims, rows), (prows, slab) = obs.shape[1], prior.shape, proj.shape
    panel, part = index.shape[0], index.shape[0] // n_row
    parts = max(1, LANES // sims)
    width = parts * math.gcd(UNIT, rows // parts)
    halves = 2
    size = math.gcd(slab, UNIT)
    units = slab // size
    chips, pairs = n_col // 2, n_row // 2
    all_sims, pb, hs, pieces = n_col * sims, prows // n_row, sims // 2, 2 * chips
    back = 2 * (chips - 1)
    chunks = 8 if units % 8 == 0 else units
    n_keep, n_far = D3 + 2, 2 * (D3 - D2) + 2
    start = min(EARLY, units // 4)
    hold, lent, stock = max(2, start + 1), max(SENDS, start), max(3, start + 2)
    vmem, anywhere = pl.BlockSpec(memory_space=pltpu.VMEM), pl.BlockSpec(memory_space=pltpu.HBM)
    dma, bf16, f32 = pltpu.SemaphoreType.DMA, jnp.bfloat16, jnp.float32
    return pl.pallas_call(
        functools.partial(stream_kernel, n_row, n_col, units),
        in_specs=[vmem] + [anywhere] * 5,
        out_specs=[vmem, vmem],
        out_shape=[jax.ShapeDtypeStruct((sims, rows), f32), jax.ShapeDtypeStruct((sims, pb), f32)],
        scratch_shapes=[
            pltpu.VMEM((rows // width, sims, width), bf16),
            pltpu.VMEM((rows // parts, parts * sims), f32),
            pltpu.VMEM((panel // LANES, LANES), jnp.int32),
            pltpu.SMEM((panel // LANES, LANES), jnp.int32),
            pltpu.VMEM((part, parts * sims), f32),
            pltpu.VMEM((n_row, halves, sims // halves, part), bf16),
            pltpu.VMEM((halves, n_row - 1, sims // halves, part), bf16),
            pltpu.VMEM((halves, sims // halves, part), bf16),
            pltpu.VMEM((n_row, halves, sims // halves, part), bf16),
            pltpu.VMEM((all_sims, depth), bf16),
            pltpu.VMEM((rows // LANES, LANES), f32),
            pltpu.VMEM((stock, n_col, size, depth), bf16),
            pltpu.VMEM((stock, n_col, sims, size), f32),
            pltpu.VMEM((3, prows, size), bf16),
            pltpu.VMEM((hold, chips, all_sims, size), f32),
            pltpu.VMEM((hold, chips, all_sims, size), f32),
            pltpu.VMEM((n_keep, chips, all_sims, size), f32),
            pltpu.VMEM((n_keep, chips - 1, sims, size), f32),
            pltpu.VMEM((n_keep, sims, size), f32),
            pltpu.VMEM((lent, chips - 1, all_sims, size), bf16),
            pltpu.VMEM((n_far, chips - 1, all_sims, size), bf16),
            pltpu.VMEM((all_sims, size), bf16),
            pltpu.VMEM((all_sims, prows), f32),
            pltpu.VMEM((back, units, sims, size), bf16),
            pltpu.VMEM((back, units, sims, size), bf16),
            pltpu.VMEM((pieces, hs, prows), f32),
            pltpu.VMEM((pieces, 2, pairs, hs, pb), f32),
            pltpu.VMEM((pieces, pairs, hs, pb), f32),
            pltpu.VMEM((pieces, pairs, hs, pb), f32),
            pltpu.VMEM((pieces, pairs - 1, hs, pb), f32),
            pltpu.VMEM((pieces, hs, pb), f32),
            pltpu.VMEM((pieces, hs, pb), f32),
            pltpu.SemaphoreType.REGULAR, dma((rows // width,)), dma, dma((halves, n_row - 1)), dma((halves, n_row - 1)), dma((halves, n_row)), dma((halves, n_row)),
            dma, dma((stock, n_col)), dma((stock, n_col)), dma((3,)), dma((hold,)), dma((hold,)),
            dma((max(1, start), 2)), dma((max(1, start), 2)),
            dma((lent, chips - 1)), dma((n_far, chips - 1)),
            dma((max(1, start), 2, chips - 1)), dma((max(1, start), 2, chips - 1)),
            dma((n_keep, chips - 1)), dma((units, chips - 1)), dma((n_keep,)), dma((units,)),
            dma((chunks, back)), dma((chunks, back)),
            dma((pieces,)), dma((pieces,)), dma((pieces,)), dma((pieces,)),
            dma((pieces, pairs - 1)), dma((pieces, pairs - 1)), dma((pieces,)), dma((pieces,)),
        ],
        compiler_params=pltpu.CompilerParams(has_side_effects=True, collective_id=0, vmem_limit_bytes=LIMIT),
        name="stream",
    )(index.reshape(panel // LANES, LANES), *[pltpu.with_memory_space_constraint(x, pltpu.HBM) for x in (maps, apod.reshape(rows // LANES, LANES), obs, prior, proj)])


def emit_kernel(out_ref, pout_ref, out, pout, sem):
    rows, wide = out_ref.shape[0] // EMIT_ROWS, out_ref.shape[1] // EMIT_COLS
    copies = [pltpu.make_async_copy(pout_ref, pout, sem.at[0])]
    for i in range(EMIT_ROWS):
        for j in range(EMIT_COLS):
            at = (slice(i * rows, (i + 1) * rows), slice(j * wide, (j + 1) * wide))
            copies.append(pltpu.make_async_copy(out_ref.at[at], out.at[at], sem.at[len(copies)]))
    for cp in copies:
        cp.start()
    for cp in copies:
        cp.wait()


def emit(out, pout):
    vmem, hbm = pl.BlockSpec(memory_space=pltpu.VMEM), pl.BlockSpec(memory_space=pltpu.HBM)
    return pl.pallas_call(
        emit_kernel,
        out_shape=[jax.ShapeDtypeStruct(x.shape, x.dtype) for x in (out, pout)],
        in_specs=[vmem] * 2,
        out_specs=[hbm] * 2,
        scratch_shapes=[pltpu.SemaphoreType.DMA((EMIT_ROWS * EMIT_COLS + 1,))],
        compiler_params=pltpu.CompilerParams(vmem_limit_bytes=8 * 1024 * 1024),
        name="emit",
    )(out, pout)


def on_device(n_row, n_col, obs_panel, skies, panel_index, prior_sum, apod, proj_panel):
    out, projection = emit(*stream(panel_index, skies.T, obs_panel, prior_sum.T, apod, proj_panel, n_row, n_col))
    return out.T, projection.T


def solution(mesh):
    in_specs = (P("row", "col"), P("row", "col"), P(), P("row", "col"), P("row"), P(None, ("row", "col")))
    out_specs = (P("row", "col"), P("row", "col"))
    body = functools.partial(on_device, mesh.shape["row"], mesh.shape["col"])
    return jax.shard_map(body, mesh=mesh, in_specs=in_specs, out_specs=out_specs, check_vma=False)
```
